32 devices in a mesh: mem: 4 (over y, core), patch: 8 (over z, x).
Axes of the slice: x: 2, y: 2, z: 4, core: 2. Of those that a mesh axis runs over, the one named last changes fastest.
Arguments:
- mesh_latent: bfloat16 [4, 4096, 512], P('mem', 'patch'), may hold values from -6 to 6
- edge_latent: bfloat16 [8192, 512], P('patch'), may hold values from -6 to 6
- grid_edge_latent: bfloat16 [12288, 512], P('patch'), may hold values from -6 to 6
- edge_inner: bfloat16 [1536, 512], replicated, may hold values from -0.15625 to 0.15625
- edge_outer: bfloat16 [512, 512], replicated, may hold values from -0.25 to 0.25
- node_inner: bfloat16 [1024, 512], replicated, may hold values from -0.1875 to 0.1875
- node_outer: bfloat16 [512, 512], replicated, may hold values from -0.25 to 0.25
- grid_inner: bfloat16 [1024, 512], replicated, may hold values from -0.1875 to 0.1875
- grid_outer: bfloat16 [512, 512], replicated, may hold values from -0.25 to 0.25
- out_weight: bfloat16 [87, 512], replicated, may hold values from -0.25 to 0.25
- prior_state: float32 [87, 4096], P(None, 'patch'), may hold values from -6 to 6
- target: float32 [87, 4096], P(None, 'patch'), may hold values from -6 to 6
- channel_weight: float32 [87], replicated, may hold values from 0.2 to 2
- area_weight: float32 [4096], P('patch'), may hold values from 0.2 to 2
- send_rows: int32 [8, 2, 96], P('patch'), may hold values from 0 to 511
- edge_senders: int32 [8192], P('patch'), may hold values from 0 to 703, as said below
- edge_receivers: int32 [8192], P('patch'), may hold values from 0 to 511
- edge_count: int32 [8], P('patch'), may hold values from 256 to 1024, as said below
- grid_senders: int32 [12288], P('patch'), may hold values from 0 to 703, as said below
Outputs:
- crps_gradient: float32 [4, 87, 4096], P('mem', None, 'patch')
The draws below stay inside these ranges and needn't reach their ends.
Inputs may be any that keep to these rules, and one draw needn't show every extreme that they name: `edge_senders`: values below 512 name a row of the band itself, values from 512 to 607 a row received from the previous band, larger values a row received from the next band; the first band names none of the second kind and the last band none of the third. `grid_senders`: as for edge_senders: own rows, rows from the previous band, rows from the next band; the first and last bands name only bands that exist. The live slots of a band are its first edge_count slots; some band has all 1024 slots live.
All inputs are finite; a program needn't handle non-finite values.
Results may differ from the reference program's by a relative error of at most 0.023.
Values may be sent and summed in bfloat16 or wider, within the bound.
No kernel may reach another device: no remote copies, remote signals or barrier semaphores. Data moves between devices by JAX's collectives and lax.ppermute only.
A program may use at most 64 MiB of HBM per device.

```python
import math
import jax
import jax.numpy as jnp
from jax import lax

D = 512
C = 87
NODE_DEV = 512
EDGE_DEV = 1024
DEC_DEV = 1536
HALO = 96
MEMBERS = 4
NODES = 4096
EDGES = 8192
DEC_EDGES = 12288
GRID = 4096
N_PATCH = 8


def pick_senders(key, slots):
    region = jax.random.randint(jax.random.fold_in(key, 1), (N_PATCH, slots), 0, 10)
    own_rows = jax.random.randint(jax.random.fold_in(key, 2), (N_PATCH, slots), 0, NODE_DEV)
    halo_rows = jax.random.randint(jax.random.fold_in(key, 3), (N_PATCH, slots), 0, HALO)
    patch_index = jnp.arange(N_PATCH)[:, None]
    lower = (region >= 6) & (region < 8) & (patch_index > 0)
    upper = (region >= 8) & (patch_index < N_PATCH - 1)
    chosen = jnp.where(lower, NODE_DEV + halo_rows, jnp.where(upper, NODE_DEV + HALO + halo_rows, own_rows))
    return chosen.reshape(-1).astype(jnp.int32)


def draw_edge_senders(key, part):
    return pick_senders(jax.random.fold_in(key, 11), EDGE_DEV)


def draw_grid_senders(key, part):
    return pick_senders(jax.random.fold_in(key, 12), DEC_DEV)


def draw_edge_count(key, part):
    counts = jax.random.randint(jax.random.fold_in(key, 21), (N_PATCH,), EDGE_DEV // 4, EDGE_DEV + 1)
    fullest = jax.random.randint(jax.random.fold_in(key, 22), (), 0, N_PATCH)
    return counts.at[fullest].set(EDGE_DEV).astype(jnp.int32)


def place_ends(array, own_key, smallest, largest):
    longest = array.shape.index(max(array.shape))
    spots = []
    for shift in (0, 1):
        where = [jax.random.randint(jax.random.fold_in(own_key, axis), (), 0, length) for axis, length in enumerate(array.shape)]
        where[longest] = (where[longest] + shift) % array.shape[longest]
        spots.append(tuple(where))
    return array.at[spots[0]].set(smallest).at[spots[1]].set(largest)


def block_scale(stream_key, dims, cuts, smallest, top_value):
    gain = 1.0
    for position, blocks in cuts:
        draws = jax.random.uniform(jax.random.fold_in(jax.random.fold_in(stream_key, 6), position), (blocks,), jnp.float32, smallest / len(cuts), top_value / len(cuts))
        gain = gain * jnp.repeat(jnp.exp(draws), dims[position] // blocks).reshape((-1,) + (1,) * (len(dims) - 1 - position))
    return gain


def bell_draw(stream_key, extent, scale, bound, cuts=(), kind=jnp.bfloat16):
    loudness = block_scale(stream_key, extent, cuts, -0.22, 0.18) if cuts else 1.0
    values = jax.random.normal(stream_key, extent, jnp.float32) * scale * loudness
    return jnp.minimum(jnp.maximum(values, -bound), bound).astype(kind)


def setup_inputs(seed: int = 0) -> dict:
    streams_of = jax.random.split(jax.random.key(seed), 20)
    return {
        "mesh_latent": bell_draw(streams_of[0], (MEMBERS, NODES, D), 1.0, 6.0, ((0, 4), (1, 8))),
        "edge_latent": bell_draw(streams_of[1], (EDGES, D), 1.0, 6.0, ((0, 8),)),
        "grid_edge_latent": bell_draw(streams_of[2], (DEC_EDGES, D), 1.0, 6.0, ((0, 8),)),
        "edge_inner": bell_draw(streams_of[3], (3 * D, D), (3 * D) ** -0.5, 0.15625),
        "edge_outer": bell_draw(streams_of[4], (D, D), D ** -0.5, 0.25),
        "node_inner": bell_draw(streams_of[5], (2 * D, D), (2 * D) ** -0.5, 0.1875),
        "node_outer": bell_draw(streams_of[6], (D, D), D ** -0.5, 0.25),
        "grid_inner": bell_draw(streams_of[7], (2 * D, D), (2 * D) ** -0.5, 0.1875),
        "grid_outer": bell_draw(streams_of[8], (D, D), D ** -0.5, 0.25),
        "out_weight": bell_draw(streams_of[9], (C, D), D ** -0.5, 0.25),
        "prior_state": bell_draw(streams_of[10], (C, GRID), 1.0, 6.0, ((1, 8),), jnp.float32),
        "target": bell_draw(streams_of[11], (C, GRID), 1.0, 6.0, ((1, 8),), jnp.float32),
        "channel_weight": jnp.clip(jnp.exp(jax.random.uniform(streams_of[12], (C,), jnp.float32, math.log(0.2), math.log(2.0))), 0.2, 2.0),
        "area_weight": jnp.clip(jnp.exp(math.log(2.0) - 2.3025851 * jax.random.uniform(streams_of[13], (GRID,), jnp.float32) ** block_scale(streams_of[13], (GRID,), ((0, 8),), -0.2, 0.2)), 0.2, 2.0),
        "send_rows": place_ends(jax.random.randint(streams_of[14], (N_PATCH, 2, HALO), 0, NODE_DEV), jax.random.fold_in(streams_of[14], 1), 0, NODE_DEV - 1).astype(jnp.int32),
        "edge_senders": draw_edge_senders(jax.random.fold_in(streams_of[19], 71), 0),
        "edge_receivers": place_ends(jax.random.randint(streams_of[16], (EDGES,), 0, NODE_DEV), jax.random.fold_in(streams_of[16], 1), 0, NODE_DEV - 1).astype(jnp.int32),
        "edge_count": draw_edge_count(jax.random.fold_in(streams_of[19], 71), 0),
        "grid_senders": draw_grid_senders(jax.random.fold_in(streams_of[19], 71), 0),
    }


epsilon = 1e-05
smooth = 0.25

def layer_norm(values):
    average = lax.optimization_barrier(jnp.mean(values, -1, keepdims=True))
    centred = values - average
    spread = lax.optimization_barrier(jnp.mean(centred * centred, -1, keepdims=True))
    return centred / jnp.sqrt(spread + epsilon)

def network(inputs, inner_weight, outer_weight):
    inner = jax.nn.silu(jnp.dot(inputs, inner_weight, preferred_element_type=jnp.float32)).astype(jnp.bfloat16)
    return layer_norm(jnp.dot(inner, outer_weight, preferred_element_type=jnp.float32))

def smooth_slope(values):
    return values / jnp.sqrt(values * values + smooth * smooth)

def take_rows(table, rows):
    return table[rows]

def reference(mesh_latent, edge_latent, grid_edge_latent, edge_inner, edge_outer, node_inner, node_outer, grid_inner, grid_outer, out_weight, prior_state, target, channel_weight, area_weight, send_rows, edge_senders, edge_receivers, edge_count, grid_senders):
    gather_rows = jax.vmap(take_rows)

    def extend(latent):
        upward = gather_rows(latent, send_rows[:, 0])
        downward = gather_rows(latent, send_rows[:, 1])
        blank = jnp.zeros((1, HALO, D), latent.dtype)
        lower = jnp.concatenate([blank, upward[:-1]], 0)
        upper = jnp.concatenate([downward[1:], blank], 0)
        return jnp.concatenate([latent, lower, upper], 1)
    senders = edge_senders.reshape(N_PATCH, EDGE_DEV)
    receivers = edge_receivers.reshape(N_PATCH, EDGE_DEV)
    grid_rows = grid_senders.reshape(N_PATCH, DEC_DEV)
    live_slots = jnp.arange(EDGE_DEV, dtype=jnp.int32)[None, :] < edge_count[:, None]

    def add_rows(values, rows):
        return jax.ops.segment_sum(values, rows, NODE_DEV)

    def member(latent):
        extended = extend(latent)
        inputs = jnp.concatenate([gather_rows(extended, senders), gather_rows(latent, receivers), edge_latent.reshape(N_PATCH, EDGE_DEV, D)], 2)
        message = network(inputs.reshape(-1, 3 * D), edge_inner, edge_outer).reshape(N_PATCH, EDGE_DEV, D)
        message = jnp.where(live_slots[:, :, None], message, 0.0)
        summed = jax.vmap(add_rows)(message, receivers).astype(jnp.bfloat16)
        node_inputs = jnp.concatenate([latent, summed], 2).reshape(-1, 2 * D)
        change = network(node_inputs, node_inner, node_outer).reshape(N_PATCH, NODE_DEV, D)
        updated = (latent.astype(jnp.float32) + change).astype(jnp.bfloat16)
        grid_inputs = jnp.concatenate([gather_rows(extend(updated), grid_rows), grid_edge_latent.reshape(N_PATCH, DEC_DEV, D)], 2)
        grid_message = network(grid_inputs.reshape(-1, 2 * D), grid_inner, grid_outer)
        grid_sum = grid_message.reshape(-1, 3, D).sum(1).astype(jnp.bfloat16)
        output = lax.dot_general(out_weight, grid_sum, (((1,), (1,)), ((), ())), preferred_element_type=jnp.float32)
        return prior_state + output - target
    difference = lax.map(member, mesh_latent.reshape(MEMBERS, N_PATCH, NODE_DEV, D))

    def bracket(own_diff):
        return smooth_slope(own_diff) - lax.optimization_barrier(jnp.sum(smooth_slope(own_diff[None] - difference), 0)) / (MEMBERS - 1)
    result = lax.map(bracket, difference)
    return result * channel_weight[None, :, None] * area_weight[None, None, :]
```

```python
import jax
import jax.numpy as jnp
from jax import lax
from jax.experimental import pallas as pl
from jax.experimental.pallas import tpu as pltpu
from jax.sharding import PartitionSpec as P

epsilon = 1e-05
smooth = 0.25
LANES = 128
VMEM = pltpu.VMEM
f32 = jnp.float32
bf16 = jnp.bfloat16


def dot(a, b):
    return jnp.dot(a, b, preferred_element_type=f32)


def silu(v):
    half = 0.5 * v
    return half + half * jnp.tanh(half)


def normalised(u):
    average = jnp.mean(u, -1, keepdims=True)
    centred = u - average
    spread = jnp.mean(centred * centred, -1, keepdims=True)
    return centred * lax.rsqrt(spread + epsilon)


def column(row):
    return jnp.transpose(jnp.broadcast_to(row, (8, row.shape[1])))[:, :1]


def columns(ref, first, count):
    parts = [
        column(ref[:, first + at : first + at + LANES]) for at in range(0, count, LANES)
    ]
    return parts[0] if len(parts) == 1 else jnp.concatenate(parts, 0)


def chosen(index, width):
    lanes = lax.broadcasted_iota(jnp.int32, (index.shape[0], width), 1)
    return jnp.where(index == lanes, 1.0, 0.0).astype(bf16)


def placed(index, height):
    rows = lax.broadcasted_iota(jnp.int32, (height, index.shape[1]), 0)
    return jnp.where(index == rows, 1.0, 0.0).astype(bf16)


def halo_slots(index, nodes, halo, odd):
    at = index - nodes
    turned = jnp.where(at < halo, at + halo, at - halo)
    return jnp.where(at < 0, -1, jnp.where(odd, at, turned))


def send_columns(sends_ref, odd):
    halo = sends_ref.shape[1]
    onward, back = sends_ref[0:1, :], sends_ref[1:2, :]
    pair = jnp.where(odd, back, onward)
    cross = jnp.where(odd, onward, back)
    return column(pair), column(cross), halo


def select_kernel(odd_ref, sends_ref, table_ref, pair_ref, cross_ref):
    odd = odd_ref[0] == 1
    pair, cross, _ = send_columns(sends_ref, odd)
    nodes = table_ref.shape[0]
    pair_ref[...] = dot(chosen(pair, nodes), table_ref[...]).astype(bf16)
    cross_ref[...] = dot(chosen(cross, nodes), table_ref[...]).astype(bf16)


def edge_own_kernel(block, senders_ref, receivers_ref, table_ref, edge_ref, inner_ref, pre_ref, sent_ref, got_ref):
    nodes, width = table_ref.shape
    sent_ref[...] = dot(table_ref[...], inner_ref[0:width, :]).astype(bf16)
    got_ref[...] = dot(table_ref[...], inner_ref[width : 2 * width, :]).astype(bf16)
    for at in range(0, edge_ref.shape[0], block):
        rows = slice(at, at + block)
        total = dot(edge_ref[rows, :], inner_ref[2 * width :, :])
        total += dot(chosen(columns(senders_ref, at, block), nodes), sent_ref[...])
        total += dot(chosen(columns(receivers_ref, at, block), nodes), got_ref[...])
        pre_ref[rows, :] = total


def node_kernel(
    block,
    odd_ref,
    count_ref,
    sends_ref,
    senders_ref,
    receivers_ref,
    pre_ref,
    pair_in_ref,
    cross_in_ref,
    table_ref,
    sender_weight_ref,
    outer_ref,
    node_inner_ref,
    node_outer_ref,
    updated_ref,
    pair_ref,
    cross_ref,
    halo_ref,
):
    odd = odd_ref[0] == 1
    nodes, width = table_ref.shape
    halo = pair_in_ref.shape[0]
    halo_ref[0:halo, :] = dot(pair_in_ref[...], sender_weight_ref[...]).astype(bf16)
    halo_ref[halo:, :] = dot(cross_in_ref[...], sender_weight_ref[...]).astype(bf16)
    summed = None
    for at in range(0, pre_ref.shape[0], block):
        rows = slice(at, at + block)
        slots = halo_slots(columns(senders_ref, at, block), nodes, halo, odd)
        total = pre_ref[rows, :] + dot(chosen(slots, 2 * halo), halo_ref[...])
        message = normalised(dot(silu(total).astype(bf16), outer_ref[...])).astype(bf16)
        position = at + lax.broadcasted_iota(jnp.int32, (1, block), 1)
        target = jnp.where(position < count_ref[0], receivers_ref[:, rows], -1)
        part = dot(placed(target, nodes), message)
        summed = part if summed is None else summed + part
    pre = dot(table_ref[...], node_inner_ref[0:width, :])
    pre += dot(summed.astype(bf16), node_inner_ref[width:, :])
    change = normalised(dot(silu(pre).astype(bf16), node_outer_ref[...]))
    updated_ref[...] = (table_ref[...].astype(f32) + change).astype(bf16)
    pair, cross, _ = send_columns(sends_ref, odd)
    pair_ref[...] = dot(chosen(pair, nodes), updated_ref[...]).astype(bf16)
    cross_ref[...] = dot(chosen(cross, nodes), updated_ref[...]).astype(bf16)


def grid_own_kernel(block, senders_ref, table_ref, edge_ref, inner_ref, pre_ref, sent_ref):
    nodes, width = table_ref.shape
    sent_ref[...] = dot(table_ref[...], inner_ref[0:width, :]).astype(bf16)
    for at in range(0, edge_ref.shape[0], block):
        rows = slice(at, at + block)
        total = dot(edge_ref[rows, :], inner_ref[width:, :])
        total += dot(chosen(columns(senders_ref, at, block), nodes), sent_ref[...])
        pre_ref[rows, :] = total


def grid_kernel(
    block,
    nodes,
    odd_ref,
    senders_ref,
    pre_ref,
    pair_in_ref,
    cross_in_ref,
    sender_weight_ref,
    outer_ref,
    out_weight_ref,
    prior_ref,
    target_ref,
    difference_ref,
    rounded_ref,
    halo_ref,
):
    odd = odd_ref[0] == 1
    halo = pair_in_ref.shape[0]
    halo_ref[0:halo, :] = dot(pair_in_ref[...], sender_weight_ref[...]).astype(bf16)
    halo_ref[halo:, :] = dot(cross_in_ref[...], sender_weight_ref[...]).astype(bf16)
    points = block // 3
    first = 3 * lax.broadcasted_iota(jnp.int32, (points, block), 0)
    lanes = lax.broadcasted_iota(jnp.int32, (points, block), 1)
    adding = jnp.where((lanes >= first) & (lanes < first + 3), 1.0, 0.0).astype(bf16)
    for at in range(0, pre_ref.shape[0], block):
        rows = slice(at, at + block)
        slots = halo_slots(columns(senders_ref, at, block), nodes, halo, odd)
        total = pre_ref[rows, :] + dot(chosen(slots, 2 * halo), halo_ref[...])
        message = normalised(dot(silu(total).astype(bf16), outer_ref[...])).astype(bf16)
        grid_sum = dot(adding, message).astype(bf16)
        output = lax.dot_general(
            out_weight_ref[...], grid_sum, (((1,), (1,)), ((), ())), preferred_element_type=f32
        )
        spots = slice(at // 3, at // 3 + points)
        difference = prior_ref[:, spots] + output - target_ref[:, spots]
        difference_ref[:, spots] = difference
        rounded_ref[:, spots] = difference.astype(bf16)


def smooth_slope(values):
    return values * lax.rsqrt(values * values + smooth * smooth)


def score_kernel(channel_ref, area_ref, difference_ref, everyone_ref, out_ref):
    difference = difference_ref[...]
    members = everyone_ref.shape[0]
    pairwise = smooth_slope(difference - everyone_ref[0].astype(f32))
    for n in range(1, members):
        pairwise += smooth_slope(difference - everyone_ref[n].astype(f32))
    result = smooth_slope(difference) - pairwise / (members - 1)
    weight = jnp.transpose(jnp.broadcast_to(channel_ref[...], (8, channel_ref.shape[1])))[:, :1]
    out_ref[:, 0, :] = result * weight * area_ref[...]


def spec():
    return pl.BlockSpec(memory_space=VMEM)


def scalar():
    return pl.BlockSpec(memory_space=pltpu.SMEM)


def shape(*dims, dtype=bf16):
    return jax.ShapeDtypeStruct(dims, dtype)


def call(kernel, name, scalars, operands, outs, scratch, flops):
    moved = sum(o.size * o.dtype.itemsize for o in (*operands, *outs))
    return pl.pallas_call(
        kernel,
        name=name,
        out_shape=outs,
        in_specs=[scalar()] * len(scalars) + [spec()] * len(operands),
        out_specs=tuple(spec() for _ in outs),
        scratch_shapes=scratch,
        cost_estimate=pl.CostEstimate(flops=flops, bytes_accessed=moved, transcendentals=0),
    )(*scalars, *operands)


def exchange(pair_rows, cross_rows):
    bands = lax.axis_size("patch")
    pair = [(i, i ^ 1) for i in range(bands) if i ^ 1 < bands]
    other = [((i + 1) ^ 1) - 1 for i in range(bands)]
    cross = [(i, j) for i, j in enumerate(other) if 0 <= j < bands]
    return lax.ppermute(pair_rows, "patch", pair), lax.ppermute(cross_rows, "patch", cross)


def per_device(
    mesh_latent,
    edge_latent,
    grid_edge_latent,
    edge_inner,
    edge_outer,
    node_inner,
    node_outer,
    grid_inner,
    grid_outer,
    out_weight,
    prior_state,
    target,
    channel_weight,
    area_weight,
    send_rows,
    edge_senders,
    edge_receivers,
    edge_count,
    grid_senders,
):
    latent = mesh_latent[0]
    sends = send_rows[0]
    halo = sends.shape[1]
    nodes, width = latent.shape
    edges = edge_senders.shape[0]
    grid_edges = grid_senders.shape[0]
    channels, points = prior_state.shape
    odd = (lax.axis_index("patch") % 2).astype(jnp.int32)[None]
    senders = edge_senders[None]
    receivers = edge_receivers[None]
    grid_rows = grid_senders[None]
    block = 256
    grid_block = 384

    pair, cross = call(
        select_kernel, "select", (odd,), (sends, latent), (shape(halo, width), shape(halo, width)), (), 10**8
    )
    pair_in, cross_in = exchange(pair, cross)
    (pre,) = call(
        lambda *refs: edge_own_kernel(block, *refs),
        "edge_own",
        (),
        (senders, receivers, latent, edge_latent, edge_inner),
        (shape(edges, width, dtype=f32),),
        (VMEM((nodes, width), bf16), VMEM((nodes, width), bf16)),
        2 * 10**9,
    )
    updated, pair, cross = call(
        lambda *refs: node_kernel(block, *refs),
        "node",
        (odd, edge_count),
        (
            sends,
            senders,
            receivers,
            pre,
            pair_in,
            cross_in,
            latent,
            edge_inner[:width],
            edge_outer,
            node_inner,
            node_outer,
        ),
        (shape(nodes, width), shape(halo, width), shape(halo, width)),
        (VMEM((2 * halo, width), bf16),),
        2 * 10**9,
    )
    pair_in, cross_in = exchange(pair, cross)
    (pre,) = call(
        lambda *refs: grid_own_kernel(grid_block, *refs),
        "grid_own",
        (),
        (grid_rows, updated, grid_edge_latent, grid_inner),
        (shape(grid_edges, width, dtype=f32),),
        (VMEM((nodes, width), bf16),),
        2 * 10**9,
    )
    difference, rounded = call(
        lambda *refs: grid_kernel(grid_block, nodes, *refs),
        "grid",
        (odd,),
        (
            grid_rows,
            pre,
            pair_in,
            cross_in,
            grid_inner[:width],
            grid_outer,
            out_weight,
            prior_state,
            target,
        ),
        (shape(channels, points, dtype=f32), shape(channels, points)),
        (VMEM((2 * halo, width), bf16),),
        2 * 10**9,
    )
    everyone = lax.all_gather(rounded[None], "mem", axis=0, tiled=True)
    (gradient,) = call(
        score_kernel,
        "score",
        (),
        (channel_weight[None], area_weight[None], difference, everyone),
        (shape(channels, 1, points, dtype=f32),),
        (),
        10**7,
    )
    return jnp.transpose(gradient, (1, 0, 2))


def solution(mesh):
    in_specs = (
        P("mem", "patch", None),
        P("patch", None),
        P("patch", None),
        P(),
        P(),
        P(),
        P(),
        P(),
        P(),
        P(),
        P(None, "patch"),
        P(None, "patch"),
        P(),
        P("patch"),
        P("patch", None, None),
        P("patch"),
        P("patch"),
        P("patch"),
        P("patch"),
    )
    out_specs = P("mem", None, "patch")
    return jax.shard_map(
        per_device, mesh=mesh, in_specs=in_specs, out_specs=out_specs, check_vma=False
    )
```

```python
import jax
import jax.numpy as jnp
from jax import lax
from jax.experimental import pallas as pl
from jax.experimental.pallas import tpu as pltpu
from jax.sharding import PartitionSpec as P

epsilon = 1e-05
smooth = 0.25
LANES = 128
VMEM = pltpu.VMEM
f32 = jnp.float32
bf16 = jnp.bfloat16


def dot(a, b):
    return jnp.dot(a, b, preferred_element_type=f32)


def silu_of_twice(half):
    return (half + half * jnp.tanh(half)).astype(bf16)


def normalised(centred):
    spread = jnp.mean(centred * centred, -1, keepdims=True)
    return centred * lax.rsqrt(spread + epsilon)


def centred_weight(ref):
    weight = ref[...].astype(f32)
    return (weight - jnp.mean(weight, -1, keepdims=True)).astype(bf16)


def column(row):
    return jnp.transpose(jnp.broadcast_to(row, (8, row.shape[1])))[:, :1]


def columns(ref, first, count):
    parts = [
        column(ref[first + at : first + at + LANES][None]) for at in range(0, count, LANES)
    ]
    return parts[0] if len(parts) == 1 else jnp.concatenate(parts, 0)


def chosen(index, width):
    lanes = lax.broadcasted_iota(jnp.int32, (index.shape[0], width), 1)
    return jnp.where(index == lanes, 1.0, 0.0).astype(bf16)


def placed(index, height):
    rows = lax.broadcasted_iota(jnp.int32, (height, index.shape[1]), 0)
    return jnp.where(index == rows, 1.0, 0.0).astype(bf16)


def halo_slots(index, nodes, halo, odd):
    at = index - nodes
    turned = jnp.where(at < halo, at + halo, at - halo)
    return jnp.where(at < 0, -1, jnp.where(odd, at, turned))


def pick_sends(sends_ref, odd, table, pair_ref, cross_ref):
    halo = sends_ref.shape[1]
    onward, back = sends_ref[0:1, :], sends_ref[1:2, :]
    pair = jnp.where(odd, back, onward)
    cross = jnp.where(odd, onward, back)
    index = jnp.concatenate([column(pair), column(cross)], 0)
    rows = dot(chosen(index, table.shape[0]), table).astype(bf16)
    pair_ref[...] = rows[:halo]
    cross_ref[...] = rows[halo:]


def halo_projection(pair_ref, cross_ref, weight_ref):
    rows = jnp.concatenate([pair_ref[...], cross_ref[...]], 0)
    return (0.5 * dot(rows, weight_ref[0 : rows.shape[1], :])).astype(bf16)


def select_kernel(odd_ref, sends_hbm, table_hbm, pair_ref, cross_ref, sends_ref, table_ref, semaphores):
    copies = [
        pltpu.make_async_copy(sends_hbm, sends_ref, semaphores.at[0]),
        pltpu.make_async_copy(table_hbm, table_ref, semaphores.at[1]),
    ]
    for copy in copies:
        copy.start()
    for copy in copies:
        copy.wait()
    pick_sends(sends_ref, odd_ref[0] == 1, table_ref[...], pair_ref, cross_ref)


def edge_own_kernel(
    block,
    senders_ref,
    receivers_ref,
    table_ref,
    edge_ref,
    inner_ref,
    outer_ref,
    node_inner_ref,
    node_outer_ref,
    pre_ref,
    node_pre_ref,
    outer_out_ref,
    node_outer_out_ref,
    sent_ref,
    got_ref,
):
    nodes, width = table_ref.shape
    sent_ref[...] = dot(table_ref[...], inner_ref[0:width, :]).astype(bf16)
    got_ref[...] = dot(table_ref[...], inner_ref[width : 2 * width, :]).astype(bf16)
    for at in range(0, edge_ref.shape[0], block):
        rows = slice(at, at + block)
        total = dot(edge_ref[rows, :], inner_ref[2 * width :, :])
        total += dot(chosen(columns(senders_ref, at, block), nodes), sent_ref[...])
        total += dot(chosen(columns(receivers_ref, at, block), nodes), got_ref[...])
        pre_ref[rows, :] = 0.5 * total
    node_pre_ref[...] = 0.5 * dot(table_ref[...], node_inner_ref[0:width, :])
    outer_out_ref[...] = centred_weight(outer_ref)
    node_outer_out_ref[...] = centred_weight(node_outer_ref)


def node_kernel(
    block,
    odd_ref,
    count_ref,
    sends_ref,
    senders_ref,
    receivers_ref,
    pre_ref,
    pair_in_ref,
    cross_in_ref,
    table_ref,
    inner_ref,
    outer_ref,
    node_pre_ref,
    node_inner_ref,
    node_outer_ref,
    updated_ref,
    pair_ref,
    cross_ref,
    halo_ref,
):
    odd = odd_ref[0] == 1
    nodes, width = table_ref.shape
    halo = pair_in_ref.shape[0]
    halo_ref[...] = halo_projection(pair_in_ref, cross_in_ref, inner_ref)
    summed = None
    for at in range(0, pre_ref.shape[0], block):
        rows = slice(at, at + block)
        slots = halo_slots(columns(senders_ref, at, block), nodes, halo, odd)
        total = pre_ref[rows, :] + dot(chosen(slots, 2 * halo), halo_ref[...])
        message = normalised(dot(silu_of_twice(total), outer_ref[...])).astype(bf16)
        position = at + lax.broadcasted_iota(jnp.int32, (1, block), 1)
        target = jnp.where(position < count_ref[0], receivers_ref[rows][None], -1)
        part = dot(placed(target, nodes), message)
        summed = part if summed is None else summed + part
    pre = node_pre_ref[...] + dot((0.5 * summed).astype(bf16), node_inner_ref[width:, :])
    change = normalised(dot(silu_of_twice(pre), node_outer_ref[...]))
    updated = (table_ref[...].astype(f32) + change).astype(bf16)
    updated_ref[...] = updated
    pick_sends(sends_ref, odd, updated, pair_ref, cross_ref)


def grid_own_kernel(block, senders_ref, table_ref, edge_ref, inner_ref, outer_ref, pre_ref, outer_out_ref, sent_ref):
    nodes, width = table_ref.shape
    sent_ref[...] = dot(table_ref[...], inner_ref[0:width, :]).astype(bf16)
    for at in range(0, edge_ref.shape[0], block):
        rows = slice(at, at + block)
        total = dot(edge_ref[rows, :], inner_ref[width:, :])
        total += dot(chosen(columns(senders_ref, at, block), nodes), sent_ref[...])
        pre_ref[rows, :] = 0.5 * total
    outer_out_ref[...] = centred_weight(outer_ref)


def grid_kernel(
    block,
    nodes,
    odd_ref,
    senders_ref,
    pre_ref,
    pair_in_ref,
    cross_in_ref,
    inner_ref,
    outer_ref,
    out_weight_ref,
    prior_ref,
    target_ref,
    difference_ref,
    rounded_ref,
    halo_ref,
    message_ref,
):
    odd = odd_ref[0] == 1
    halo = pair_in_ref.shape[0]
    halo_ref[...] = halo_projection(pair_in_ref, cross_in_ref, inner_ref)
    points = block // 3
    for at in range(0, pre_ref.shape[0], block):
        rows = slice(at, at + block)
        slots = halo_slots(columns(senders_ref, at, block), nodes, halo, odd)
        total = pre_ref[rows, :] + dot(chosen(slots, 2 * halo), halo_ref[...])
        message = normalised(dot(silu_of_twice(total), outer_ref[...]))
        tiles = []
        for t in range(message_ref.shape[0]):
            message_ref[t, rows, :] = message[:, t * LANES : (t + 1) * LANES]
            triple = [message_ref[t, pl.ds(at + k, points, 3), :] for k in range(3)]
            tiles.append((triple[0] + triple[1] + triple[2]).astype(bf16))
        grid_sum = jnp.concatenate(tiles, 1)
        output = lax.dot_general(
            out_weight_ref[...], grid_sum, (((1,), (1,)), ((), ())), preferred_element_type=f32
        )
        spots = slice(at // 3, at // 3 + points)
        difference = prior_ref[:, spots] + output - target_ref[:, spots]
        difference_ref[:, spots] = difference
        rounded_ref[:, spots] = difference.astype(bf16)


def smooth_slope(values):
    return values * lax.rsqrt(values * values + smooth * smooth)


def score_kernel(channel_ref, area_ref, difference_ref, everyone_ref, out_ref):
    difference = difference_ref[...]
    members = everyone_ref.shape[0]
    pairwise = smooth_slope(difference - everyone_ref[0].astype(f32))
    for n in range(1, members):
        pairwise += smooth_slope(difference - everyone_ref[n].astype(f32))
    result = smooth_slope(difference) - pairwise / (members - 1)
    weight = jnp.transpose(jnp.broadcast_to(channel_ref[...], (8, channel_ref.shape[1])))[:, :1]
    out_ref[:, 0, :] = result * weight * area_ref[...]


def spec():
    return pl.BlockSpec(memory_space=VMEM)


def far():
    return pl.BlockSpec(memory_space=pltpu.HBM)


def scalar():
    return pl.BlockSpec(memory_space=pltpu.SMEM)


def shape(*dims, dtype=bf16):
    return jax.ShapeDtypeStruct(dims, dtype)


def call(kernel, name, scalars, operands, outs, scratch, flops, from_hbm=False):
    moved = sum(o.size * o.dtype.itemsize for o in (*operands, *outs))
    return pl.pallas_call(
        kernel,
        name=name,
        out_shape=outs,
        in_specs=[scalar()] * len(scalars) + [far() if from_hbm else spec()] * len(operands),
        out_specs=tuple(spec() for _ in outs),
        scratch_shapes=scratch,
        compiler_params=pltpu.CompilerParams(vmem_limit_bytes=24 * 2**20),
        cost_estimate=pl.CostEstimate(flops=flops, bytes_accessed=moved, transcendentals=0),
    )(*scalars, *operands)


def exchange(pair_rows, cross_rows):
    members, bands = lax.axis_size("mem"), lax.axis_size("patch")
    pair = [(i, i ^ 1) for i in range(bands)]
    cross = []
    for m in range(members):
        for i in range(bands):
            j = ((i + 1) ^ 1) - 1
            other = (m, j) if 0 <= j < bands else (m ^ 1, i)
            cross.append((m * bands + i, other[0] * bands + other[1]))
    crossed = lax.ppermute(cross_rows, ("mem", "patch"), cross)
    return lax.ppermute(pair_rows, "patch", pair), crossed


def per_device(
    mesh_latent,
    edge_latent,
    grid_edge_latent,
    edge_inner,
    edge_outer,
    node_inner,
    node_outer,
    grid_inner,
    grid_outer,
    out_weight,
    prior_state,
    target,
    channel_weight,
    area_weight,
    send_rows,
    edge_senders,
    edge_receivers,
    edge_count,
    grid_senders,
):
    latent = mesh_latent[0]
    sends = send_rows[0]
    halo = sends.shape[1]
    nodes, width = latent.shape
    edges = edge_senders.shape[0]
    grid_edges = grid_senders.shape[0]
    channels, points = prior_state.shape
    odd = (lax.axis_index("patch") % 2).astype(jnp.int32)[None]
    senders = edge_senders
    receivers = edge_receivers
    grid_rows = grid_senders
    block = 512
    grid_block = 768

    pair, cross = call(
        select_kernel,
        "select",
        (odd,),
        tuple(pltpu.with_memory_space_constraint(x, pltpu.HBM) for x in (sends, latent)),
        (shape(halo, width), shape(halo, width)),
        (VMEM((2, halo), jnp.int32), VMEM((nodes, width), bf16), pltpu.SemaphoreType.DMA((2,))),
        10**10,
        from_hbm=True,
    )
    pair_in, cross_in = exchange(pair, cross)
    pre, node_pre, outer, second = call(
        lambda *refs: edge_own_kernel(block, *refs),
        "edge_own",
        (),
        (senders, receivers, latent, edge_latent, edge_inner, edge_outer, node_inner, node_outer),
        (
            shape(edges, width, dtype=f32),
            shape(nodes, width, dtype=f32),
            shape(width, width),
            shape(width, width),
        ),
        (VMEM((nodes, width), bf16), VMEM((nodes, width), bf16)),
        10**10,
    )
    updated, pair, cross = call(
        lambda *refs: node_kernel(block, *refs),
        "node",
        (odd, edge_count),
        (
            sends,
            senders,
            receivers,
            pre,
            pair_in,
            cross_in,
            latent,
            edge_inner,
            outer,
            node_pre,
            node_inner,
            second,
        ),
        (shape(nodes, width), shape(halo, width), shape(halo, width)),
        (VMEM((2 * halo, width), bf16),),
        10**10,
    )
    pair_in, cross_in = exchange(pair, cross)
    pre, outer = call(
        lambda *refs: grid_own_kernel(grid_block, *refs),
        "grid_own",
        (),
        (grid_rows, updated, grid_edge_latent, grid_inner, grid_outer),
        (shape(grid_edges, width, dtype=f32), shape(width, width)),
        (VMEM((nodes, width), bf16),),
        10**10,
    )
    difference, rounded = call(
        lambda *refs: grid_kernel(grid_block, nodes, *refs),
        "grid",
        (odd,),
        (grid_rows, pre, pair_in, cross_in, grid_inner, outer, out_weight, prior_state, target),
        (shape(channels, points, dtype=f32), shape(channels, points)),
        (VMEM((2 * halo, width), bf16), VMEM((width // LANES, grid_edges, LANES), f32)),
        10**10,
    )
    everyone = lax.all_gather(rounded[None], "mem", axis=0, tiled=True)
    (gradient,) = call(
        score_kernel,
        "score",
        (),
        (channel_weight[None], area_weight[None], difference, everyone),
        (shape(channels, 1, points, dtype=f32),),
        (),
        10**7,
    )
    return jnp.transpose(gradient, (1, 0, 2))


def solution(mesh):
    in_specs = (
        P("mem", "patch", None),
        P("patch", None),
        P("patch", None),
        P(),
        P(),
        P(),
        P(),
        P(),
        P(),
        P(),
        P(None, "patch"),
        P(None, "patch"),
        P(),
        P("patch"),
        P("patch", None, None),
        P("patch"),
        P("patch"),
        P("patch"),
        P("patch"),
    )
    out_specs = P("mem", None, "patch")
    return jax.shard_map(
        per_device, mesh=mesh, in_specs=in_specs, out_specs=out_specs, check_vma=False
    )
```

```python
import jax
import jax.numpy as jnp
from jax import lax
from jax.experimental import pallas as pl
from jax.experimental.pallas import tpu as pltpu
from jax.sharding import PartitionSpec as P

epsilon = 1e-05
smooth = 0.25
LANES = 128
VMEM = pltpu.VMEM
f32 = jnp.float32
bf16 = jnp.bfloat16


def dot(a, b):
    return jnp.dot(a, b, preferred_element_type=f32)


def silu_of_twice(half):
    return (half + half * jnp.tanh(half)).astype(bf16)


def normalised(centred):
    spread = jnp.mean(centred * centred, -1, keepdims=True)
    return centred * lax.rsqrt(spread + epsilon)


def centred_weight(ref):
    weight = ref[...].astype(f32)
    return (weight - jnp.mean(weight, -1, keepdims=True)).astype(bf16)


def column(row):
    return jnp.transpose(jnp.broadcast_to(row, (8, row.shape[1])))[:, :1]


def columns(ref, first, count):
    parts = [
        column(ref[first + at : first + at + LANES][None]) for at in range(0, count, LANES)
    ]
    return parts[0] if len(parts) == 1 else jnp.concatenate(parts, 0)


def chosen(index, width):
    lanes = lax.broadcasted_iota(jnp.int32, (index.shape[0], width), 1)
    return jnp.where(index == lanes, 1.0, 0.0).astype(bf16)


def placed(index, height):
    rows = lax.broadcasted_iota(jnp.int32, (height, index.shape[1]), 0)
    return jnp.where(index == rows, 1.0, 0.0).astype(bf16)


def halo_slots(index, nodes, halo, odd):
    at = index - nodes
    turned = jnp.where(at < halo, at + halo, at - halo)
    return jnp.where(at < 0, -1, jnp.where(odd, at, turned))


def halo_choice(senders_ref, nodes, halo, odd, choice_ref):
    for at in range(0, senders_ref.shape[0], LANES):
        slots = halo_slots(senders_ref[at : at + LANES][None], nodes, halo, odd)
        choice_ref[at : at + LANES, :] = chosen(column(slots), choice_ref.shape[1])


def send_index(sends_ref, odd):
    onward, back = sends_ref[0:1, :], sends_ref[1:2, :]
    return jnp.where(odd, back, onward), jnp.where(odd, onward, back)


def halo_projection(pair_ref, cross_ref, weight_ref):
    rows = jnp.concatenate([pair_ref[...], cross_ref[...]], 0)
    return (0.5 * dot(rows, weight_ref[0 : rows.shape[1], :])).astype(bf16)


def select_kernel(odd_ref, sends_hbm, table_hbm, pair_ref, cross_ref, sends_ref, table_ref, semaphores):
    pieces = semaphores.shape[0] - 1
    step = table_ref.shape[0] // pieces
    first = pltpu.make_async_copy(sends_hbm, sends_ref, semaphores.at[pieces])
    first.start()
    copies = []
    for at in range(pieces):
        rows = pl.ds(at * step, step)
        copies.append(
            pltpu.make_async_copy(table_hbm.at[rows, :], table_ref.at[rows, :], semaphores.at[at])
        )
        copies[-1].start()
    first.wait()
    pair, cross = send_index(sends_ref, odd_ref[0] == 1)
    index = jnp.concatenate([column(pair), column(cross)], 0)
    picked = None
    for at, copy in enumerate(copies):
        copy.wait()
        part = dot(chosen(index - at * step, step), table_ref[at * step : (at + 1) * step, :])
        picked = part if picked is None else picked + part
    halo = pair_ref.shape[0]
    rows = picked.astype(bf16)
    pair_ref[...] = rows[:halo]
    cross_ref[...] = rows[halo:]


def edge_own_kernel(
    block,
    odd_ref,
    count_ref,
    sends_ref,
    senders_ref,
    receivers_ref,
    pair_ref,
    cross_ref,
    table_ref,
    edge_ref,
    inner_ref,
    outer_ref,
    node_inner_ref,
    node_outer_ref,
    pre_ref,
    sent_pre_ref,
    outer_out_ref,
    node_outer_out_ref,
    choice_ref,
    placing_ref,
    sent_placing_ref,
    sent_ref,
    got_ref,
):
    nodes, width = table_ref.shape
    edges = edge_ref.shape[0]
    halo = pair_ref.shape[0]
    odd = odd_ref[0] == 1
    sent_ref[...] = dot(table_ref[...], inner_ref[0:width, :]).astype(bf16)
    got_ref[...] = dot(table_ref[...], inner_ref[width : 2 * width, :]).astype(bf16)
    for at in range(0, edges, block):
        rows = slice(at, at + block)
        total = dot(edge_ref[rows, :], inner_ref[2 * width :, :])
        total += dot(chosen(columns(senders_ref, at, block), nodes), sent_ref[...])
        total += dot(chosen(columns(receivers_ref, at, block), nodes), got_ref[...])
        pre_ref[rows, :] = 0.5 * total
    outer_out_ref[...] = centred_weight(outer_ref)
    node_outer_out_ref[...] = centred_weight(node_outer_ref)
    halo_choice(senders_ref, nodes, halo, odd, choice_ref)
    position = lax.broadcasted_iota(jnp.int32, (1, edges), 1)
    target = jnp.where(position < count_ref[...][None], receivers_ref[...][None], -1)
    placing_ref[...] = placed(target, nodes)
    pair, cross = send_index(sends_ref, odd)
    index = jnp.concatenate([column(pair), column(cross)], 0)
    sent_placing_ref[...] = jnp.where(index == target, 1.0, 0.0).astype(bf16)
    rows = jnp.concatenate([pair_ref[...], cross_ref[...]], 0)
    sent_pre_ref[...] = 0.5 * dot(rows, node_inner_ref[0:width, :])


def node_update(placing_ref, message, table, pre, node_inner_ref, node_outer_ref):
    width = table.shape[1]
    summed = dot(placing_ref[...], message)
    pre = pre + dot((0.5 * summed).astype(bf16), node_inner_ref[width:, :])
    change = normalised(dot(silu_of_twice(pre), node_outer_ref[...]))
    return (table.astype(f32) + change).astype(bf16)


def message_kernel(
    block,
    choice_ref,
    sent_placing_ref,
    pre_ref,
    pair_in_ref,
    cross_in_ref,
    pair_ref,
    cross_ref,
    inner_ref,
    outer_ref,
    sent_pre_ref,
    node_inner_ref,
    node_outer_ref,
    message_ref,
    pair_out_ref,
    cross_out_ref,
    halo_ref,
):
    halo = pair_ref.shape[0]
    halo_ref[...] = halo_projection(pair_in_ref, cross_in_ref, inner_ref)
    for at in range(0, pre_ref.shape[0], block):
        rows = slice(at, at + block)
        total = pre_ref[rows, :] + dot(choice_ref[rows, :], halo_ref[...])
        message_ref[rows, :] = normalised(dot(silu_of_twice(total), outer_ref[...])).astype(bf16)
    table = jnp.concatenate([pair_ref[...], cross_ref[...]], 0)
    updated = node_update(
        sent_placing_ref, message_ref[...], table, sent_pre_ref[...], node_inner_ref, node_outer_ref
    )
    pair_out_ref[...] = updated[:halo]
    cross_out_ref[...] = updated[halo:]


def grid_own_kernel(
    block,
    halo,
    odd_ref,
    senders_ref,
    placing_ref,
    message_ref,
    table_ref,
    node_inner_ref,
    node_outer_ref,
    edge_ref,
    inner_ref,
    outer_ref,
    pre_ref,
    outer_out_ref,
    choice_ref,
    sent_ref,
):
    nodes, width = table_ref.shape
    table = table_ref[...]
    pre = 0.5 * dot(table, node_inner_ref[0:width, :])
    updated = node_update(placing_ref, message_ref[...], table, pre, node_inner_ref, node_outer_ref)
    sent_ref[...] = dot(updated, inner_ref[0:width, :]).astype(bf16)
    for at in range(0, edge_ref.shape[0], block):
        rows = slice(at, at + block)
        total = dot(edge_ref[rows, :], inner_ref[width:, :])
        total += dot(chosen(columns(senders_ref, at, block), nodes), sent_ref[...])
        pre_ref[rows, :] = 0.5 * total
    outer_out_ref[...] = centred_weight(outer_ref)
    halo_choice(senders_ref, nodes, halo, odd_ref[0] == 1, choice_ref)


def grid_kernel(
    block,
    choice_ref,
    pre_ref,
    pair_in_ref,
    cross_in_ref,
    inner_ref,
    outer_ref,
    out_weight_ref,
    prior_ref,
    target_ref,
    difference_ref,
    rounded_ref,
    halo_ref,
    message_ref,
):
    halo_ref[...] = halo_projection(pair_in_ref, cross_in_ref, inner_ref)
    points = block // 3
    for at in range(0, pre_ref.shape[0], block):
        rows = slice(at, at + block)
        total = pre_ref[rows, :] + dot(choice_ref[rows, :], halo_ref[...])
        message = normalised(dot(silu_of_twice(total), outer_ref[...]))
        tiles = []
        for t in range(message_ref.shape[0]):
            message_ref[t, rows, :] = message[:, t * LANES : (t + 1) * LANES]
            triple = [message_ref[t, pl.ds(at + k, points, 3), :] for k in range(3)]
            tiles.append((triple[0] + triple[1] + triple[2]).astype(bf16))
        grid_sum = jnp.concatenate(tiles, 1)
        output = lax.dot_general(
            out_weight_ref[...], grid_sum, (((1,), (1,)), ((), ())), preferred_element_type=f32
        )
        spots = slice(at // 3, at // 3 + points)
        difference = prior_ref[:, spots] + output - target_ref[:, spots]
        difference_ref[:, spots] = difference
        rounded_ref[:, spots] = difference.astype(bf16)


def smooth_slope(values):
    return values * lax.rsqrt(values * values + smooth * smooth)


def score_kernel(channel_ref, area_ref, difference_ref, *refs):
    *others, partial_ref, weight_ref = refs
    difference = difference_ref[...]
    members = 2 * len(others)
    pairwise = smooth_slope(difference - difference)
    for other_ref in others:
        pairwise += smooth_slope(difference - other_ref[...].astype(f32))
    channel = jnp.broadcast_to(channel_ref[...], (8, channel_ref.shape[1]))
    weight = jnp.transpose(channel)[:, :1] * area_ref[...]
    partial_ref[...] = (smooth_slope(difference) - pairwise / (members - 1)) * weight
    weight_ref[...] = weight / (members - 1)


def finish_kernel(difference_ref, partial_ref, weight_ref, *refs):
    *others, out_ref = refs
    difference = difference_ref[...]
    pairwise = None
    for other_ref in others:
        part = smooth_slope(difference - other_ref[...].astype(f32))
        pairwise = part if pairwise is None else pairwise + part
    out_ref[:, 0, :] = partial_ref[...] - pairwise * weight_ref[...]


def spec():
    return pl.BlockSpec(memory_space=VMEM)


def far():
    return pl.BlockSpec(memory_space=pltpu.HBM)


def scalar():
    return pl.BlockSpec(memory_space=pltpu.SMEM)


def shape(*dims, dtype=bf16):
    return jax.ShapeDtypeStruct(dims, dtype)


def call(kernel, name, scalars, operands, outs, scratch, flops, from_hbm=False):
    moved = sum(o.size * o.dtype.itemsize for o in (*operands, *outs))
    return pl.pallas_call(
        kernel,
        name=name,
        out_shape=outs,
        in_specs=[scalar()] * len(scalars) + [far() if from_hbm else spec()] * len(operands),
        out_specs=tuple(spec() for _ in outs),
        scratch_shapes=scratch,
        compiler_params=pltpu.CompilerParams(vmem_limit_bytes=24 * 2**20),
        cost_estimate=pl.CostEstimate(flops=flops, bytes_accessed=moved, transcendentals=0),
    )(*scalars, *operands)


def exchange(pair_rows, cross_rows):
    members, bands = lax.axis_size("mem"), lax.axis_size("patch")
    pair = [(i, i ^ 1) for i in range(bands)]
    cross = []
    for m in range(members):
        for i in range(bands):
            j = ((i + 1) ^ 1) - 1
            other = (m, j) if 0 <= j < bands else (m ^ 1, i)
            cross.append((m * bands + i, other[0] * bands + other[1]))
    crossed = lax.ppermute(cross_rows, ("mem", "patch"), cross)
    return lax.ppermute(pair_rows, "patch", pair), crossed


def mate(rows):
    members = lax.axis_size("mem")
    return lax.ppermute(rows, "mem", [(m, m ^ 1) for m in range(members)])


def chip_mates(rows):
    members = lax.axis_size("mem")
    far_own = [
        lax.ppermute(rows, "mem", [(m, (m + shift) % members) for m in range(members)])
        for shift in range(2, members, 2)
    ]
    return mate(rows), far_own


def per_device(
    mesh_latent,
    edge_latent,
    grid_edge_latent,
    edge_inner,
    edge_outer,
    node_inner,
    node_outer,
    grid_inner,
    grid_outer,
    out_weight,
    prior_state,
    target,
    channel_weight,
    area_weight,
    send_rows,
    edge_senders,
    edge_receivers,
    edge_count,
    grid_senders,
):
    latent = mesh_latent[0]
    sends = send_rows[0]
    halo = sends.shape[1]
    nodes, width = latent.shape
    edges = edge_senders.shape[0]
    grid_edges = grid_senders.shape[0]
    channels, points = prior_state.shape
    odd = (lax.axis_index("patch") % 2).astype(jnp.int32)[None]
    senders = edge_senders
    receivers = edge_receivers
    grid_rows = grid_senders

    pair, cross = call(
        select_kernel,
        "select",
        (odd,),
        tuple(pltpu.with_memory_space_constraint(x, pltpu.HBM) for x in (sends, latent)),
        (shape(halo, width), shape(halo, width)),
        (VMEM((2, halo), jnp.int32), VMEM((nodes, width), bf16), pltpu.SemaphoreType.DMA((3,))),
        10**10,
        from_hbm=True,
    )
    pair_in, cross_in = exchange(pair, cross)
    pre, sent_pre, outer, second, choice, placing, sent_placing = call(
        lambda *refs: edge_own_kernel(edges // 2, *refs),
        "edge_own",
        (odd,),
        (
            edge_count,
            sends,
            senders,
            receivers,
            pair,
            cross,
            latent,
            edge_latent,
            edge_inner,
            edge_outer,
            node_inner,
            node_outer,
        ),
        (
            shape(edges, width, dtype=f32),
            shape(2 * halo, width, dtype=f32),
            shape(width, width),
            shape(width, width),
            shape(edges, 2 * halo),
            shape(nodes, edges),
            shape(2 * halo, edges),
        ),
        (VMEM((nodes, width), bf16), VMEM((nodes, width), bf16)),
        10**10,
    )
    message, pair, cross = call(
        lambda *refs: message_kernel(edges, *refs),
        "message",
        (),
        (
            choice,
            sent_placing,
            pre,
            pair_in,
            cross_in,
            pair,
            cross,
            edge_inner,
            outer,
            sent_pre,
            node_inner,
            second,
        ),
        (shape(edges, width), shape(halo, width), shape(halo, width)),
        (VMEM((2 * halo, width), bf16),),
        10**10,
    )
    pair_in, cross_in = exchange(pair, cross)
    pre, outer, choice = call(
        lambda *refs: grid_own_kernel(grid_edges // 2, halo, *refs),
        "grid_own",
        (odd,),
        (
            grid_rows,
            placing,
            message,
            latent,
            node_inner,
            second,
            grid_edge_latent,
            grid_inner,
            grid_outer,
        ),
        (shape(grid_edges, width, dtype=f32), shape(width, width), shape(grid_edges, 2 * halo)),
        (VMEM((nodes, width), bf16),),
        10**10,
    )
    difference, rounded = call(
        lambda *refs: grid_kernel(grid_edges, *refs),
        "grid",
        (),
        (choice, pre, pair_in, cross_in, grid_inner, outer, out_weight, prior_state, target),
        (shape(channels, points, dtype=f32), shape(channels, points)),
        (VMEM((2 * halo, width), bf16), VMEM((width // LANES, grid_edges, LANES), f32)),
        10**10,
    )
    near, far_own = chip_mates(rounded)
    partial, weight = call(
        score_kernel,
        "score",
        (),
        (channel_weight[None], area_weight[None], difference, near, *far_own),
        (shape(channels, points, dtype=f32), shape(channels, points, dtype=f32)),
        (),
        10**8,
    )
    (gradient,) = call(
        finish_kernel,
        "finish",
        (),
        (difference, partial, weight, *(mate(rows) for rows in far_own)),
        (shape(channels, 1, points, dtype=f32),),
        (),
        10**7,
    )
    return jnp.transpose(gradient, (1, 0, 2))


def solution(mesh):
    in_specs = (
        P("mem", "patch", None),
        P("patch", None),
        P("patch", None),
        P(),
        P(),
        P(),
        P(),
        P(),
        P(),
        P(),
        P(None, "patch"),
        P(None, "patch"),
        P(),
        P("patch"),
        P("patch", None, None),
        P("patch"),
        P("patch"),
        P("patch"),
        P("patch"),
    )
    out_specs = P("mem", None, "patch")
    return jax.shard_map(
        per_device, mesh=mesh, in_specs=in_specs, out_specs=out_specs, check_vma=False
    )
```

```python
import jax
import jax.numpy as jnp
from jax import lax
from jax.experimental import pallas as pl
from jax.experimental.pallas import tpu as pltpu
from jax.sharding import PartitionSpec as P

epsilon = 1e-05
smooth = 0.25
LANES = 128
VMEM = pltpu.VMEM
f32 = jnp.float32
bf16 = jnp.bfloat16


def dot(a, b):
    return jnp.dot(a, b, preferred_element_type=f32)


def silu_of_twice(half):
    return (half + half * jnp.tanh(half)).astype(bf16)


def normalised(centred):
    spread = jnp.mean(centred * centred, -1, keepdims=True)
    return centred * lax.rsqrt(spread + epsilon)


def centred_weight(ref):
    weight = ref[...].astype(f32)
    return (weight - jnp.mean(weight, -1, keepdims=True)).astype(bf16)


def column(row):
    return jnp.transpose(jnp.broadcast_to(row, (8, row.shape[1])))[:, :1]


def columns(ref, first, count):
    parts = [
        column(ref[first + at : first + at + LANES][None]) for at in range(0, count, LANES)
    ]
    return parts[0] if len(parts) == 1 else jnp.concatenate(parts, 0)


def chosen(index, width):
    lanes = lax.broadcasted_iota(jnp.int32, (index.shape[0], width), 1)
    return jnp.where(index == lanes, 1.0, 0.0).astype(bf16)


def placed(index, height):
    rows = lax.broadcasted_iota(jnp.int32, (height, index.shape[1]), 0)
    return jnp.where(index == rows, 1.0, 0.0).astype(bf16)


def halo_slots(index, nodes, halo, odd):
    at = index - nodes
    turned = jnp.where(at < halo, at + halo, at - halo)
    return jnp.where(at < 0, -1, jnp.where(odd, at, turned))


def halo_choice(senders_ref, nodes, halo, odd, choice_ref):
    for at in range(0, senders_ref.shape[0], LANES):
        slots = halo_slots(senders_ref[at : at + LANES][None], nodes, halo, odd)
        choice_ref[at : at + LANES, :] = chosen(column(slots), choice_ref.shape[1])


def send_index(sends_ref, odd):
    onward, back = sends_ref[0:1, :], sends_ref[1:2, :]
    return jnp.where(odd, back, onward), jnp.where(odd, onward, back)


def halo_projection(pair_ref, cross_ref, weight_ref):
    rows = jnp.concatenate([pair_ref[...], cross_ref[...]], 0)
    return (0.5 * dot(rows, weight_ref[0 : rows.shape[1], :])).astype(bf16)


def select_kernel(odd_ref, sends_hbm, table_hbm, pair_ref, cross_ref, sends_ref, table_ref, semaphores):
    pieces = semaphores.shape[0] - 1
    step = table_ref.shape[0] // pieces
    first = pltpu.make_async_copy(sends_hbm, sends_ref, semaphores.at[pieces])
    first.start()
    copies = []
    for at in range(pieces):
        rows = pl.ds(at * step, step)
        copies.append(
            pltpu.make_async_copy(table_hbm.at[rows, :], table_ref.at[rows, :], semaphores.at[at])
        )
        copies[-1].start()
    first.wait()
    pair, cross = send_index(sends_ref, odd_ref[0] == 1)
    index = jnp.concatenate([column(pair), column(cross)], 0)
    picked = None
    for at, copy in enumerate(copies):
        copy.wait()
        part = dot(chosen(index - at * step, step), table_ref[at * step : (at + 1) * step, :])
        picked = part if picked is None else picked + part
    halo = pair_ref.shape[0]
    rows = picked.astype(bf16)
    pair_ref[...] = rows[:halo]
    cross_ref[...] = rows[halo:]


def edge_own_kernel(
    block,
    odd_ref,
    count_ref,
    sends_ref,
    senders_ref,
    receivers_ref,
    pair_ref,
    cross_ref,
    table_ref,
    edge_ref,
    inner_ref,
    outer_ref,
    node_inner_ref,
    node_outer_ref,
    pre_ref,
    sent_pre_ref,
    outer_out_ref,
    node_outer_out_ref,
    choice_ref,
    live_ref,
    sent_placing_ref,
    sent_ref,
    got_ref,
):
    nodes, width = table_ref.shape
    edges = edge_ref.shape[0]
    halo = pair_ref.shape[0]
    odd = odd_ref[0] == 1
    outer_out_ref[...] = centred_weight(outer_ref)
    node_outer_out_ref[...] = centred_weight(node_outer_ref)
    halo_choice(senders_ref, nodes, halo, odd, choice_ref)
    position = lax.broadcasted_iota(jnp.int32, (1, edges), 1)
    target = jnp.where(position < count_ref[...][None], receivers_ref[...][None], -1)
    live_ref[...] = target
    pair, cross = send_index(sends_ref, odd)
    index = jnp.concatenate([column(pair), column(cross)], 0)
    sent_placing_ref[...] = jnp.where(index == target, 1.0, 0.0).astype(bf16)
    sent_ref[...] = dot(table_ref[...], inner_ref[0:width, :]).astype(bf16)
    got_ref[...] = dot(table_ref[...], inner_ref[width : 2 * width, :]).astype(bf16)
    for at in range(0, edges, block):
        rows = slice(at, at + block)
        total = dot(edge_ref[rows, :], inner_ref[2 * width :, :])
        total += dot(chosen(columns(senders_ref, at, block), nodes), sent_ref[...])
        total += dot(chosen(columns(receivers_ref, at, block), nodes), got_ref[...])
        pre_ref[rows, :] = 0.5 * total
    rows = jnp.concatenate([pair_ref[...], cross_ref[...]], 0)
    sent_pre_ref[...] = 0.5 * dot(rows, node_inner_ref[0:width, :])


def node_update(placing, message, table, pre, node_inner_ref, node_outer_ref):
    width = table.shape[1]
    summed = dot(placing, message)
    pre = pre + dot((0.5 * summed).astype(bf16), node_inner_ref[width:, :])
    change = normalised(dot(silu_of_twice(pre), node_outer_ref[...]))
    return (table.astype(f32) + change).astype(bf16)


def message_kernel(
    block,
    choice_ref,
    sent_placing_ref,
    pre_ref,
    pair_in_ref,
    cross_in_ref,
    pair_ref,
    cross_ref,
    inner_ref,
    outer_ref,
    sent_pre_ref,
    node_inner_ref,
    node_outer_ref,
    message_ref,
    pair_out_ref,
    cross_out_ref,
    halo_ref,
):
    halo = pair_ref.shape[0]
    halo_ref[...] = halo_projection(pair_in_ref, cross_in_ref, inner_ref)
    for at in range(0, pre_ref.shape[0], block):
        rows = slice(at, at + block)
        total = pre_ref[rows, :] + dot(choice_ref[rows, :], halo_ref[...])
        message_ref[rows, :] = normalised(dot(silu_of_twice(total), outer_ref[...])).astype(bf16)
    table = jnp.concatenate([pair_ref[...], cross_ref[...]], 0)
    updated = node_update(
        sent_placing_ref[...], message_ref[...], table, sent_pre_ref[...], node_inner_ref, node_outer_ref
    )
    pair_out_ref[...] = updated[:halo]
    cross_out_ref[...] = updated[halo:]


def grid_own_kernel(
    block,
    halo,
    odd_ref,
    senders_ref,
    live_ref,
    message_ref,
    table_ref,
    node_inner_ref,
    node_outer_ref,
    edge_ref,
    inner_ref,
    outer_ref,
    pre_ref,
    outer_out_ref,
    choice_ref,
    sent_ref,
):
    nodes, width = table_ref.shape
    table = table_ref[...]
    pre = 0.5 * dot(table, node_inner_ref[0:width, :])
    updated = node_update(placed(live_ref[...], nodes), message_ref[...], table, pre, node_inner_ref, node_outer_ref)
    sent_ref[...] = dot(updated, inner_ref[0:width, :]).astype(bf16)
    for at in range(0, edge_ref.shape[0], block):
        rows = slice(at, at + block)
        total = dot(edge_ref[rows, :], inner_ref[width:, :])
        total += dot(chosen(columns(senders_ref, at, block), nodes), sent_ref[...])
        pre_ref[rows, :] = 0.5 * total
    outer_out_ref[...] = centred_weight(outer_ref)
    halo_choice(senders_ref, nodes, halo, odd_ref[0] == 1, choice_ref)


def grid_kernel(
    block,
    choice_ref,
    pre_ref,
    pair_in_ref,
    cross_in_ref,
    inner_ref,
    outer_ref,
    out_weight_ref,
    prior_ref,
    target_ref,
    difference_ref,
    rounded_ref,
    halo_ref,
    message_ref,
):
    halo_ref[...] = halo_projection(pair_in_ref, cross_in_ref, inner_ref)
    points = block // 3
    for at in range(0, pre_ref.shape[0], block):
        rows = slice(at, at + block)
        total = pre_ref[rows, :] + dot(choice_ref[rows, :], halo_ref[...])
        message = normalised(dot(silu_of_twice(total), outer_ref[...]))
        tiles = []
        for t in range(message_ref.shape[0]):
            message_ref[t, rows, :] = message[:, t * LANES : (t + 1) * LANES]
            triple = [message_ref[t, pl.ds(at + k, points, 3), :] for k in range(3)]
            tiles.append((triple[0] + triple[1] + triple[2]).astype(bf16))
        grid_sum = jnp.concatenate(tiles, 1)
        output = lax.dot_general(
            out_weight_ref[...], grid_sum, (((1,), (1,)), ((), ())), preferred_element_type=f32
        )
        spots = slice(at // 3, at // 3 + points)
        difference = prior_ref[:, spots] + output - target_ref[:, spots]
        difference_ref[:, spots] = difference
        rounded_ref[:, spots] = difference.astype(bf16)


def smooth_slope(values):
    return values * lax.rsqrt(values * values + smooth * smooth)


def score_kernel(channel_ref, area_ref, difference_ref, *refs):
    *others, partial_ref, weight_ref = refs
    difference = difference_ref[...]
    members = 2 * len(others)
    pairwise = smooth_slope(difference - difference)
    for other_ref in others:
        pairwise += smooth_slope(difference - other_ref[...].astype(f32))
    channel = jnp.broadcast_to(channel_ref[...], (8, channel_ref.shape[1]))
    weight = jnp.transpose(channel)[:, :1] * area_ref[...]
    partial_ref[...] = (smooth_slope(difference) - pairwise / (members - 1)) * weight
    weight_ref[...] = weight / (members - 1)


def finish_kernel(difference_ref, partial_ref, weight_ref, *refs):
    *others, out_ref = refs
    difference = difference_ref[...]
    pairwise = None
    for other_ref in others:
        part = smooth_slope(difference - other_ref[...].astype(f32))
        pairwise = part if pairwise is None else pairwise + part
    out_ref[:, 0, :] = partial_ref[...] - pairwise * weight_ref[...]


def spec():
    return pl.BlockSpec(memory_space=VMEM)


def far():
    return pl.BlockSpec(memory_space=pltpu.HBM)


def scalar():
    return pl.BlockSpec(memory_space=pltpu.SMEM)


def shape(*dims, dtype=bf16):
    return jax.ShapeDtypeStruct(dims, dtype)


def call(kernel, name, scalars, operands, outs, scratch, flops, from_hbm=False):
    moved = sum(o.size * o.dtype.itemsize for o in (*operands, *outs))
    return pl.pallas_call(
        kernel,
        name=name,
        out_shape=outs,
        in_specs=[scalar()] * len(scalars) + [far() if from_hbm else spec()] * len(operands),
        out_specs=tuple(spec() for _ in outs),
        scratch_shapes=scratch,
        compiler_params=pltpu.CompilerParams(vmem_limit_bytes=24 * 2**20),
        cost_estimate=pl.CostEstimate(flops=flops, bytes_accessed=moved, transcendentals=0),
    )(*scalars, *operands)


def exchange(pair_rows, cross_rows):
    members, bands = lax.axis_size("mem"), lax.axis_size("patch")
    pair = [(i, i ^ 1) for i in range(bands)]
    cross = []
    for m in range(members):
        for i in range(bands):
            j = ((i + 1) ^ 1) - 1
            other = (m, j) if 0 <= j < bands else (m ^ 1, i)
            cross.append((m * bands + i, other[0] * bands + other[1]))
    crossed = lax.ppermute(cross_rows, ("mem", "patch"), cross)
    return lax.ppermute(pair_rows, "patch", pair), crossed


def mate(rows):
    members = lax.axis_size("mem")
    return lax.ppermute(rows, "mem", [(m, m ^ 1) for m in range(members)])


def chip_mates(rows):
    members = lax.axis_size("mem")
    far_own = [
        lax.ppermute(rows, "mem", [(m, (m + shift) % members) for m in range(members)])
        for shift in range(2, members, 2)
    ]
    return mate(rows), far_own


def per_device(
    mesh_latent,
    edge_latent,
    grid_edge_latent,
    edge_inner,
    edge_outer,
    node_inner,
    node_outer,
    grid_inner,
    grid_outer,
    out_weight,
    prior_state,
    target,
    channel_weight,
    area_weight,
    send_rows,
    edge_senders,
    edge_receivers,
    edge_count,
    grid_senders,
):
    latent = mesh_latent[0]
    sends = send_rows[0]
    halo = sends.shape[1]
    nodes, width = latent.shape
    edges = edge_senders.shape[0]
    grid_edges = grid_senders.shape[0]
    channels, points = prior_state.shape
    odd = (lax.axis_index("patch") % 2).astype(jnp.int32)[None]
    senders = edge_senders
    receivers = edge_receivers
    grid_rows = grid_senders

    pair, cross = call(
        select_kernel,
        "select",
        (odd,),
        tuple(pltpu.with_memory_space_constraint(x, pltpu.HBM) for x in (sends, latent)),
        (shape(halo, width), shape(halo, width)),
        (VMEM((2, halo), jnp.int32), VMEM((nodes, width), bf16), pltpu.SemaphoreType.DMA((3,))),
        10**10,
        from_hbm=True,
    )
    pair_in, cross_in = exchange(pair, cross)
    pre, sent_pre, outer, second, choice, live, sent_placing = call(
        lambda *refs: edge_own_kernel(edges, *refs),
        "edge_own",
        (odd,),
        (
            edge_count,
            sends,
            senders,
            receivers,
            pair,
            cross,
            latent,
            edge_latent,
            edge_inner,
            edge_outer,
            node_inner,
            node_outer,
        ),
        (
            shape(edges, width, dtype=f32),
            shape(2 * halo, width, dtype=f32),
            shape(width, width),
            shape(width, width),
            shape(edges, 2 * halo),
            shape(1, edges, dtype=jnp.int32),
            shape(2 * halo, edges),
        ),
        (VMEM((nodes, width), bf16), VMEM((nodes, width), bf16)),
        10**10,
    )
    message, pair, cross = call(
        lambda *refs: message_kernel(edges, *refs),
        "message",
        (),
        (
            choice,
            sent_placing,
            pre,
            pair_in,
            cross_in,
            pair,
            cross,
            edge_inner,
            outer,
            sent_pre,
            node_inner,
            second,
        ),
        (shape(edges, width), shape(halo, width), shape(halo, width)),
        (VMEM((2 * halo, width), bf16),),
        10**10,
    )
    pair_in, cross_in = exchange(pair, cross)
    pre, outer, choice = call(
        lambda *refs: grid_own_kernel(grid_edges // 2, halo, *refs),
        "grid_own",
        (odd,),
        (
            grid_rows,
            live,
            message,
            latent,
            node_inner,
            second,
            grid_edge_latent,
            grid_inner,
            grid_outer,
        ),
        (shape(grid_edges, width, dtype=f32), shape(width, width), shape(grid_edges, 2 * halo)),
        (VMEM((nodes, width), bf16),),
        10**10,
    )
    difference, rounded = call(
        lambda *refs: grid_kernel(grid_edges, *refs),
        "grid",
        (),
        (choice, pre, pair_in, cross_in, grid_inner, outer, out_weight, prior_state, target),
        (shape(channels, points, dtype=f32), shape(channels, points)),
        (VMEM((2 * halo, width), bf16), VMEM((width // LANES, grid_edges, LANES), f32)),
        10**10,
    )
    near, far_own = chip_mates(rounded)
    partial, weight = call(
        score_kernel,
        "score",
        (),
        (channel_weight[None], area_weight[None], difference, near, *far_own),
        (shape(channels, points, dtype=f32), shape(channels, points, dtype=f32)),
        (),
        10**8,
    )
    (gradient,) = call(
        finish_kernel,
        "finish",
        (),
        (difference, partial, weight, *(mate(rows) for rows in far_own)),
        (shape(channels, 1, points, dtype=f32),),
        (),
        10**7,
    )
    return jnp.transpose(gradient, (1, 0, 2))


def solution(mesh):
    in_specs = (
        P("mem", "patch", None),
        P("patch", None),
        P("patch", None),
        P(),
        P(),
        P(),
        P(),
        P(),
        P(),
        P(),
        P(None, "patch"),
        P(None, "patch"),
        P(),
        P("patch"),
        P("patch", None, None),
        P("patch"),
        P("patch"),
        P("patch"),
        P("patch"),
    )
    out_specs = P("mem", None, "patch")
    return jax.shard_map(
        per_device, mesh=mesh, in_specs=in_specs, out_specs=out_specs, check_vma=False
    )
```

```python
import jax
import jax.numpy as jnp
from jax import lax
from jax.experimental import pallas as pl
from jax.experimental.pallas import tpu as pltpu
from jax.sharding import PartitionSpec as P

epsilon = 1e-05
smooth = 0.25
LANES = 128
VMEM = pltpu.VMEM
f32 = jnp.float32
bf16 = jnp.bfloat16


def dot(a, b):
    return jnp.dot(a, b, preferred_element_type=f32)


def odd_band():
    return lax.rem(lax.axis_index("patch"), 2) == 1


def silu_of_twice(half):
    return (half + half * jnp.tanh(half)).astype(bf16)


def normalised(centred):
    spread = jnp.mean(centred * centred, -1, keepdims=True)
    return centred * lax.rsqrt(spread + epsilon)


def centred_weight(ref):
    weight = ref[...].astype(f32)
    return (weight - jnp.mean(weight, -1, keepdims=True)).astype(bf16)


def column(row):
    return jnp.transpose(jnp.broadcast_to(row, (8, row.shape[1])))[:, :1]


def columns(ref, first, count):
    parts = [
        column(ref[first + at : first + at + LANES][None]) for at in range(0, count, LANES)
    ]
    return parts[0] if len(parts) == 1 else jnp.concatenate(parts, 0)


def chosen(index, width):
    lanes = lax.broadcasted_iota(jnp.int32, (index.shape[0], width), 1)
    return jnp.where(index == lanes, 1.0, 0.0).astype(bf16)


def placed(index, height):
    rows = lax.broadcasted_iota(jnp.int32, (height, index.shape[1]), 0)
    return jnp.where(index == rows, 1.0, 0.0).astype(bf16)


def halo_slots(index, nodes, halo, odd):
    at = index - nodes
    turned = jnp.where(at < halo, at + halo, at - halo)
    return jnp.where(at < 0, -1, jnp.where(odd, at, turned))


def halo_choice(senders_ref, nodes, halo, odd, choice_ref):
    for at in range(0, senders_ref.shape[0], LANES):
        slots = halo_slots(senders_ref[at : at + LANES][None], nodes, halo, odd)
        choice_ref[at : at + LANES, :] = chosen(column(slots), choice_ref.shape[1])


def send_index(sends_ref, odd):
    onward, back = sends_ref[0:1, :], sends_ref[1:2, :]
    return jnp.where(odd, back, onward), jnp.where(odd, onward, back)


def halo_projection(pair_ref, cross_ref, weight_ref):
    rows = jnp.concatenate([pair_ref[...], cross_ref[...]], 0)
    return (0.5 * dot(rows, weight_ref[0 : rows.shape[1], :])).astype(bf16)


def select_kernel(sends_hbm, table_hbm, pair_ref, cross_ref, sends_ref, table_ref, semaphores):
    pieces = semaphores.shape[0] - 1
    step = table_ref.shape[0] // pieces
    first = pltpu.make_async_copy(sends_hbm, sends_ref, semaphores.at[pieces])
    first.start()
    copies = []
    for at in range(pieces):
        rows = pl.ds(at * step, step)
        copies.append(
            pltpu.make_async_copy(table_hbm.at[rows, :], table_ref.at[rows, :], semaphores.at[at])
        )
        copies[-1].start()
    first.wait()
    pair, cross = send_index(sends_ref, odd_band())
    index = jnp.concatenate([column(pair), column(cross)], 0)
    picked = None
    for at, copy in enumerate(copies):
        copy.wait()
        part = dot(chosen(index - at * step, step), table_ref[at * step : (at + 1) * step, :])
        picked = part if picked is None else picked + part
    halo = pair_ref.shape[0]
    rows = picked.astype(bf16)
    pair_ref[...] = rows[:halo]
    cross_ref[...] = rows[halo:]


def edge_own_kernel(
    block,
    count_ref,
    sends_ref,
    senders_ref,
    receivers_ref,
    pair_ref,
    cross_ref,
    table_ref,
    edge_ref,
    inner_ref,
    outer_ref,
    node_inner_ref,
    node_outer_ref,
    pre_ref,
    sent_pre_ref,
    outer_out_ref,
    node_outer_out_ref,
    choice_ref,
    live_ref,
    sent_placing_ref,
    sent_ref,
    got_ref,
):
    nodes, width = table_ref.shape
    edges = edge_ref.shape[0]
    halo = pair_ref.shape[0]
    odd = odd_band()
    outer_out_ref[...] = centred_weight(outer_ref)
    node_outer_out_ref[...] = centred_weight(node_outer_ref)
    halo_choice(senders_ref, nodes, halo, odd, choice_ref)
    position = lax.broadcasted_iota(jnp.int32, (1, edges), 1)
    target = jnp.where(position < count_ref[...][None], receivers_ref[...][None], -1)
    live_ref[...] = target
    pair, cross = send_index(sends_ref, odd)
    index = jnp.concatenate([column(pair), column(cross)], 0)
    sent_placing_ref[...] = jnp.where(index == target, 1.0, 0.0).astype(bf16)
    sent_ref[...] = dot(table_ref[...], inner_ref[0:width, :]).astype(bf16)
    got_ref[...] = dot(table_ref[...], inner_ref[width : 2 * width, :]).astype(bf16)
    for at in range(0, edges, block):
        rows = slice(at, at + block)
        total = dot(edge_ref[rows, :], inner_ref[2 * width :, :])
        total += dot(chosen(columns(senders_ref, at, block), nodes), sent_ref[...])
        total += dot(chosen(columns(receivers_ref, at, block), nodes), got_ref[...])
        pre_ref[rows, :] = 0.5 * total
    rows = jnp.concatenate([pair_ref[...], cross_ref[...]], 0)
    sent_pre_ref[...] = 0.5 * dot(rows, node_inner_ref[0:width, :])


def node_update(placing, message, table, pre, node_inner_ref, node_outer_ref):
    width = table.shape[1]
    summed = dot(placing, message)
    pre = pre + dot((0.5 * summed).astype(bf16), node_inner_ref[width:, :])
    change = normalised(dot(silu_of_twice(pre), node_outer_ref[...]))
    return (table.astype(f32) + change).astype(bf16)


def message_kernel(
    block,
    choice_ref,
    sent_placing_ref,
    pre_ref,
    pair_in_ref,
    cross_in_ref,
    pair_ref,
    cross_ref,
    inner_ref,
    outer_ref,
    sent_pre_ref,
    node_inner_ref,
    node_outer_ref,
    message_ref,
    pair_out_ref,
    cross_out_ref,
    halo_ref,
):
    halo = pair_ref.shape[0]
    halo_ref[...] = halo_projection(pair_in_ref, cross_in_ref, inner_ref)
    for at in range(0, pre_ref.shape[0], block):
        rows = slice(at, at + block)
        total = pre_ref[rows, :] + dot(choice_ref[rows, :], halo_ref[...])
        message_ref[rows, :] = normalised(dot(silu_of_twice(total), outer_ref[...])).astype(bf16)
    table = jnp.concatenate([pair_ref[...], cross_ref[...]], 0)
    updated = node_update(
        sent_placing_ref[...], message_ref[...], table, sent_pre_ref[...], node_inner_ref, node_outer_ref
    )
    pair_out_ref[...] = updated[:halo]
    cross_out_ref[...] = updated[halo:]


def grid_own_kernel(
    block,
    halo,
    senders_ref,
    live_ref,
    message_ref,
    table_ref,
    node_inner_ref,
    node_outer_ref,
    edge_ref,
    inner_ref,
    outer_ref,
    pre_ref,
    outer_out_ref,
    choice_ref,
    sent_ref,
):
    nodes, width = table_ref.shape
    table = table_ref[...]
    pre = 0.5 * dot(table, node_inner_ref[0:width, :])
    updated = node_update(placed(live_ref[...], nodes), message_ref[...], table, pre, node_inner_ref, node_outer_ref)
    sent_ref[...] = dot(updated, inner_ref[0:width, :]).astype(bf16)
    for at in range(0, edge_ref.shape[0], block):
        rows = slice(at, at + block)
        total = dot(edge_ref[rows, :], inner_ref[width:, :])
        total += dot(chosen(columns(senders_ref, at, block), nodes), sent_ref[...])
        pre_ref[rows, :] = 0.5 * total
    outer_out_ref[...] = centred_weight(outer_ref)
    halo_choice(senders_ref, nodes, halo, odd_band(), choice_ref)


def grid_kernel(
    block,
    choice_ref,
    pre_ref,
    pair_in_ref,
    cross_in_ref,
    inner_ref,
    outer_ref,
    out_weight_ref,
    prior_ref,
    target_ref,
    difference_ref,
    rounded_ref,
    halo_ref,
    message_ref,
):
    halo_ref[...] = halo_projection(pair_in_ref, cross_in_ref, inner_ref)
    points = block // 3
    for at in range(0, pre_ref.shape[0], block):
        rows = slice(at, at + block)
        total = pre_ref[rows, :] + dot(choice_ref[rows, :], halo_ref[...])
        message = normalised(dot(silu_of_twice(total), outer_ref[...]))
        tiles = []
        for t in range(message_ref.shape[0]):
            message_ref[t, rows, :] = message[:, t * LANES : (t + 1) * LANES]
            triple = [message_ref[t, pl.ds(at + k, points, 3), :] for k in range(3)]
            tiles.append((triple[0] + triple[1] + triple[2]).astype(bf16))
        grid_sum = jnp.concatenate(tiles, 1)
        output = lax.dot_general(
            out_weight_ref[...], grid_sum, (((1,), (1,)), ((), ())), preferred_element_type=f32
        )
        spots = slice(at // 3, at // 3 + points)
        difference = prior_ref[:, spots] + output - target_ref[:, spots]
        difference_ref[:, spots] = difference
        rounded_ref[:, spots] = difference.astype(bf16)


def smooth_slope(values):
    return values * lax.rsqrt(values * values + smooth * smooth)


def score_kernel(channel_ref, area_ref, difference_ref, *refs):
    *others, partial_ref, weight_ref = refs
    difference = difference_ref[...]
    members = 2 * len(others)
    pairwise = smooth_slope(difference - difference)
    for other_ref in others:
        pairwise += smooth_slope(difference - other_ref[...].astype(f32))
    channel = jnp.broadcast_to(channel_ref[...], (8, channel_ref.shape[1]))
    weight = jnp.transpose(channel)[:, :1] * area_ref[...]
    partial_ref[...] = (smooth_slope(difference) - pairwise / (members - 1)) * weight
    weight_ref[...] = weight / (members - 1)


def finish_kernel(difference_ref, partial_ref, weight_ref, *refs):
    *others, out_ref = refs
    difference = difference_ref[...]
    pairwise = None
    for other_ref in others:
        part = smooth_slope(difference - other_ref[...].astype(f32))
        pairwise = part if pairwise is None else pairwise + part
    out_ref[:, 0, :] = partial_ref[...] - pairwise * weight_ref[...]


def spec():
    return pl.BlockSpec(memory_space=VMEM)


def far():
    return pl.BlockSpec(memory_space=pltpu.HBM)


def scalar():
    return pl.BlockSpec(memory_space=pltpu.SMEM)


def shape(*dims, dtype=bf16):
    return jax.ShapeDtypeStruct(dims, dtype)


def call(kernel, name, scalars, operands, outs, scratch, flops, from_hbm=False):
    moved = sum(o.size * o.dtype.itemsize for o in (*operands, *outs))
    return pl.pallas_call(
        kernel,
        name=name,
        out_shape=outs,
        in_specs=[scalar()] * len(scalars) + [far() if from_hbm else spec()] * len(operands),
        out_specs=tuple(spec() for _ in outs),
        scratch_shapes=scratch,
        compiler_params=pltpu.CompilerParams(vmem_limit_bytes=24 * 2**20),
        cost_estimate=pl.CostEstimate(flops=flops, bytes_accessed=moved, transcendentals=0),
    )(*scalars, *operands)


def exchange(pair_rows, cross_rows):
    members, bands = lax.axis_size("mem"), lax.axis_size("patch")
    pair = [(i, i ^ 1) for i in range(bands)]
    cross = []
    for m in range(members):
        for i in range(bands):
            j = ((i + 1) ^ 1) - 1
            other = (m, j) if 0 <= j < bands else (m ^ 1, i)
            cross.append((m * bands + i, other[0] * bands + other[1]))
    crossed = lax.ppermute(cross_rows, ("mem", "patch"), cross)
    return lax.ppermute(pair_rows, "patch", pair), crossed


def mate(rows):
    members = lax.axis_size("mem")
    return lax.ppermute(rows, "mem", [(m, m ^ 1) for m in range(members)])


def chip_mates(rows):
    members = lax.axis_size("mem")
    far_own = [
        lax.ppermute(rows, "mem", [(m, (m + shift) % members) for m in range(members)])
        for shift in range(2, members, 2)
    ]
    return mate(rows), far_own


def per_device(
    mesh_latent,
    edge_latent,
    grid_edge_latent,
    edge_inner,
    edge_outer,
    node_inner,
    node_outer,
    grid_inner,
    grid_outer,
    out_weight,
    prior_state,
    target,
    channel_weight,
    area_weight,
    send_rows,
    edge_senders,
    edge_receivers,
    edge_count,
    grid_senders,
):
    latent = mesh_latent[0]
    sends = send_rows[0]
    halo = sends.shape[1]
    nodes, width = latent.shape
    edges = edge_senders.shape[0]
    grid_edges = grid_senders.shape[0]
    channels, points = prior_state.shape
    senders = edge_senders
    receivers = edge_receivers
    grid_rows = grid_senders

    pair, cross = call(
        select_kernel,
        "select",
        (),
        tuple(pltpu.with_memory_space_constraint(x, pltpu.HBM) for x in (sends, latent)),
        (shape(halo, width), shape(halo, width)),
        (VMEM((2, halo), jnp.int32), VMEM((nodes, width), bf16), pltpu.SemaphoreType.DMA((3,))),
        10**10,
        from_hbm=True,
    )
    pair_in, cross_in = exchange(pair, cross)
    pre, sent_pre, outer, second, choice, live, sent_placing = call(
        lambda *refs: edge_own_kernel(edges, *refs),
        "edge_own",
        (),
        (
            edge_count,
            sends,
            senders,
            receivers,
            pair,
            cross,
            latent,
            edge_latent,
            edge_inner,
            edge_outer,
            node_inner,
            node_outer,
        ),
        (
            shape(edges, width, dtype=f32),
            shape(2 * halo, width, dtype=f32),
            shape(width, width),
            shape(width, width),
            shape(edges, 2 * halo),
            shape(1, edges, dtype=jnp.int32),
            shape(2 * halo, edges),
        ),
        (VMEM((nodes, width), bf16), VMEM((nodes, width), bf16)),
        10**10,
    )
    message, pair, cross = call(
        lambda *refs: message_kernel(edges, *refs),
        "message",
        (),
        (
            choice,
            sent_placing,
            pre,
            pair_in,
            cross_in,
            pair,
            cross,
            edge_inner,
            outer,
            sent_pre,
            node_inner,
            second,
        ),
        (shape(edges, width), shape(halo, width), shape(halo, width)),
        (VMEM((2 * halo, width), bf16),),
        10**10,
    )
    pair_in, cross_in = exchange(pair, cross)
    pre, outer, choice = call(
        lambda *refs: grid_own_kernel(grid_edges // 2, halo, *refs),
        "grid_own",
        (),
        (
            grid_rows,
            live,
            message,
            latent,
            node_inner,
            second,
            grid_edge_latent,
            grid_inner,
            grid_outer,
        ),
        (shape(grid_edges, width, dtype=f32), shape(width, width), shape(grid_edges, 2 * halo)),
        (VMEM((nodes, width), bf16),),
        10**10,
    )
    difference, rounded = call(
        lambda *refs: grid_kernel(grid_edges, *refs),
        "grid",
        (),
        (choice, pre, pair_in, cross_in, grid_inner, outer, out_weight, prior_state, target),
        (shape(channels, points, dtype=f32), shape(channels, points)),
        (VMEM((2 * halo, width), bf16), VMEM((width // LANES, grid_edges, LANES), f32)),
        10**10,
    )
    near, far_own = chip_mates(rounded)
    partial, weight = call(
        score_kernel,
        "score",
        (),
        (channel_weight[None], area_weight[None], difference, near, *far_own),
        (shape(channels, points, dtype=f32), shape(channels, points, dtype=f32)),
        (),
        10**8,
    )
    (gradient,) = call(
        finish_kernel,
        "finish",
        (),
        (difference, partial, weight, *(mate(rows) for rows in far_own)),
        (shape(channels, 1, points, dtype=f32),),
        (),
        10**7,
    )
    return jnp.transpose(gradient, (1, 0, 2))


def solution(mesh):
    in_specs = (
        P("mem", "patch", None),
        P("patch", None),
        P("patch", None),
        P(),
        P(),
        P(),
        P(),
        P(),
        P(),
        P(),
        P(None, "patch"),
        P(None, "patch"),
        P(),
        P("patch"),
        P("patch", None, None),
        P("patch"),
        P("patch"),
        P("patch"),
        P("patch"),
    )
    out_specs = P("mem", None, "patch")
    return jax.shard_map(
        per_device, mesh=mesh, in_specs=in_specs, out_specs=out_specs, check_vma=False
    )
```

```python
import jax
import jax.numpy as jnp
from jax import lax
from jax.experimental import pallas as pl
from jax.experimental.pallas import tpu as pltpu
from jax.sharding import PartitionSpec as P

epsilon = 1e-05
smooth = 0.25
LANES = 128
VMEM = pltpu.VMEM
f32 = jnp.float32
bf16 = jnp.bfloat16


def dot(a, b):
    return jnp.dot(a, b, preferred_element_type=f32)


def odd_band():
    return lax.rem(lax.axis_index("patch"), 2) == 1


def silu_of_twice(half):
    return (half + half * jnp.tanh(half)).astype(bf16)


def normalised(centred):
    spread = jnp.mean(centred * centred, -1, keepdims=True)
    return centred * lax.rsqrt(spread + epsilon)


def centred_weight(ref):
    weight = ref[...].astype(f32)
    return (weight - jnp.mean(weight, -1, keepdims=True)).astype(bf16)


def column(row):
    return jnp.transpose(jnp.broadcast_to(row, (8, row.shape[1])))[:, :1]


def columns(ref, first, count):
    parts = [
        column(ref[first + at : first + at + LANES][None]) for at in range(0, count, LANES)
    ]
    return parts[0] if len(parts) == 1 else jnp.concatenate(parts, 0)


def chosen(index, width):
    lanes = lax.broadcasted_iota(jnp.int32, (index.shape[0], width), 1)
    return jnp.where(index == lanes, 1.0, 0.0).astype(bf16)


def placed(index, height):
    rows = lax.broadcasted_iota(jnp.int32, (height, index.shape[1]), 0)
    return jnp.where(index == rows, 1.0, 0.0).astype(bf16)


def halo_slots(index, nodes, halo, odd):
    at = index - nodes
    turned = jnp.where(at < halo, at + halo, at - halo)
    return jnp.where(at < 0, -1, jnp.where(odd, at, turned))


def halo_choice(senders_ref, nodes, halo, odd, choice_ref):
    for at in range(0, senders_ref.shape[0], LANES):
        slots = halo_slots(senders_ref[at : at + LANES][None], nodes, halo, odd)
        choice_ref[at : at + LANES, :] = chosen(column(slots), choice_ref.shape[1])


def send_index(sends_ref, odd):
    onward, back = sends_ref[0:1, :], sends_ref[1:2, :]
    return jnp.where(odd, back, onward), jnp.where(odd, onward, back)


def halo_projection(pair_ref, cross_ref, weight_ref):
    rows = jnp.concatenate([pair_ref[...], cross_ref[...]], 0)
    return (0.5 * dot(rows, weight_ref[0 : rows.shape[1], :])).astype(bf16)


def select_kernel(sends_hbm, table_hbm, pair_ref, cross_ref, sends_ref, table_ref, semaphores):
    pieces = semaphores.shape[0] - 1
    step = table_ref.shape[0] // pieces
    first = pltpu.make_async_copy(sends_hbm, sends_ref, semaphores.at[pieces])
    first.start()
    copies = []
    for at in range(pieces):
        rows = pl.ds(at * step, step)
        copies.append(
            pltpu.make_async_copy(table_hbm.at[rows, :], table_ref.at[rows, :], semaphores.at[at])
        )
        copies[-1].start()
    first.wait()
    pair, cross = send_index(sends_ref, odd_band())
    index = jnp.concatenate([column(pair), column(cross)], 0)
    picked = None
    for at, copy in enumerate(copies):
        copy.wait()
        part = dot(chosen(index - at * step, step), table_ref[at * step : (at + 1) * step, :])
        picked = part if picked is None else picked + part
    halo = pair_ref.shape[0]
    rows = picked.astype(bf16)
    pair_ref[...] = rows[:halo]
    cross_ref[...] = rows[halo:]


def edge_own_kernel(
    block,
    count_ref,
    sends_ref,
    senders_ref,
    receivers_ref,
    pair_ref,
    cross_ref,
    table_ref,
    edge_ref,
    inner_ref,
    outer_ref,
    node_inner_ref,
    node_outer_ref,
    pre_ref,
    sent_pre_ref,
    outer_out_ref,
    node_outer_out_ref,
    choice_ref,
    live_ref,
    sent_placing_ref,
    sent_ref,
    got_ref,
):
    nodes, width = table_ref.shape
    edges = edge_ref.shape[0]
    halo = pair_ref.shape[0]
    odd = odd_band()
    outer_out_ref[...] = centred_weight(outer_ref)
    node_outer_out_ref[...] = centred_weight(node_outer_ref)
    halo_choice(senders_ref, nodes, halo, odd, choice_ref)
    position = lax.broadcasted_iota(jnp.int32, (1, edges), 1)
    target = jnp.where(position < count_ref[...][None], receivers_ref[...][None], -1)
    live_ref[...] = target
    pair, cross = send_index(sends_ref, odd)
    index = jnp.concatenate([column(pair), column(cross)], 0)
    sent_placing_ref[...] = jnp.where(index == target, 1.0, 0.0).astype(bf16)
    sent_ref[...] = dot(table_ref[...], inner_ref[0:width, :]).astype(bf16)
    got_ref[...] = dot(table_ref[...], inner_ref[width : 2 * width, :]).astype(bf16)
    for at in range(0, edges, block):
        rows = slice(at, at + block)
        total = dot(edge_ref[rows, :], inner_ref[2 * width :, :])
        total += dot(chosen(columns(senders_ref, at, block), nodes), sent_ref[...])
        total += dot(chosen(columns(receivers_ref, at, block), nodes), got_ref[...])
        pre_ref[rows, :] = 0.5 * total
    rows = jnp.concatenate([pair_ref[...], cross_ref[...]], 0)
    sent_pre_ref[...] = 0.5 * dot(rows, node_inner_ref[0:width, :])


def node_update(placing, message, table, pre, node_inner_ref, node_outer_ref):
    width = table.shape[1]
    summed = dot(placing, message)
    pre = pre + dot((0.5 * summed).astype(bf16), node_inner_ref[width:, :])
    change = normalised(dot(silu_of_twice(pre), node_outer_ref[...]))
    return (table.astype(f32) + change).astype(bf16)


def message_kernel(
    block,
    choice_ref,
    sent_placing_ref,
    pre_ref,
    pair_in_ref,
    cross_in_ref,
    pair_ref,
    cross_ref,
    inner_ref,
    outer_ref,
    sent_pre_ref,
    node_inner_ref,
    node_outer_ref,
    nodes_ref,
    message_ref,
    pair_out_ref,
    cross_out_ref,
    node_pre_ref,
    halo_ref,
):
    halo = pair_ref.shape[0]
    halo_ref[...] = halo_projection(pair_in_ref, cross_in_ref, inner_ref)
    for at in range(0, pre_ref.shape[0], block):
        rows = slice(at, at + block)
        total = pre_ref[rows, :] + dot(choice_ref[rows, :], halo_ref[...])
        message_ref[rows, :] = normalised(dot(silu_of_twice(total), outer_ref[...])).astype(bf16)
    table = jnp.concatenate([pair_ref[...], cross_ref[...]], 0)
    updated = node_update(
        sent_placing_ref[...], message_ref[...], table, sent_pre_ref[...], node_inner_ref, node_outer_ref
    )
    pair_out_ref[...] = updated[:halo]
    cross_out_ref[...] = updated[halo:]
    width = nodes_ref.shape[1]
    node_pre_ref[...] = 0.5 * dot(nodes_ref[...], node_inner_ref[0:width, :])


def grid_own_kernel(
    block,
    halo,
    senders_ref,
    live_ref,
    message_ref,
    table_ref,
    node_pre_ref,
    node_inner_ref,
    node_outer_ref,
    edge_ref,
    inner_ref,
    outer_ref,
    pre_ref,
    outer_out_ref,
    choice_ref,
    sent_ref,
):
    nodes, width = table_ref.shape
    table = table_ref[...]
    pre = node_pre_ref[...]
    updated = node_update(placed(live_ref[...], nodes), message_ref[...], table, pre, node_inner_ref, node_outer_ref)
    sent_ref[...] = dot(updated, inner_ref[0:width, :]).astype(bf16)
    for at in range(0, edge_ref.shape[0], block):
        rows = slice(at, at + block)
        total = dot(edge_ref[rows, :], inner_ref[width:, :])
        total += dot(chosen(columns(senders_ref, at, block), nodes), sent_ref[...])
        pre_ref[rows, :] = 0.5 * total
    outer_out_ref[...] = centred_weight(outer_ref)
    halo_choice(senders_ref, nodes, halo, odd_band(), choice_ref)


def grid_kernel(
    block,
    choice_ref,
    pre_ref,
    pair_in_ref,
    cross_in_ref,
    inner_ref,
    outer_ref,
    out_weight_ref,
    prior_ref,
    target_ref,
    difference_ref,
    rounded_ref,
    halo_ref,
    message_ref,
):
    halo_ref[...] = halo_projection(pair_in_ref, cross_in_ref, inner_ref)
    points = block // 3
    for at in range(0, pre_ref.shape[0], block):
        rows = slice(at, at + block)
        total = pre_ref[rows, :] + dot(choice_ref[rows, :], halo_ref[...])
        message = normalised(dot(silu_of_twice(total), outer_ref[...]))
        tiles = []
        for t in range(message_ref.shape[0]):
            message_ref[t, rows, :] = message[:, t * LANES : (t + 1) * LANES]
            triple = [message_ref[t, pl.ds(at + k, points, 3), :] for k in range(3)]
            tiles.append((triple[0] + triple[1] + triple[2]).astype(bf16))
        grid_sum = jnp.concatenate(tiles, 1)
        output = lax.dot_general(
            out_weight_ref[...], grid_sum, (((1,), (1,)), ((), ())), preferred_element_type=f32
        )
        spots = slice(at // 3, at // 3 + points)
        difference = prior_ref[:, spots] + output - target_ref[:, spots]
        difference_ref[:, spots] = difference
        rounded_ref[:, spots] = difference.astype(bf16)


def smooth_slope(values):
    return values * lax.rsqrt(values * values + smooth * smooth)


def score_kernel(channel_ref, area_ref, difference_ref, *refs):
    *others, partial_ref, weight_ref = refs
    difference = difference_ref[...]
    members = 2 * len(others)
    pairwise = smooth_slope(difference - difference)
    for other_ref in others:
        pairwise += smooth_slope(difference - other_ref[...].astype(f32))
    channel = jnp.broadcast_to(channel_ref[...], (8, channel_ref.shape[1]))
    weight = jnp.transpose(channel)[:, :1] * area_ref[...]
    partial_ref[...] = (smooth_slope(difference) - pairwise / (members - 1)) * weight
    weight_ref[...] = weight / (members - 1)


def finish_kernel(difference_ref, partial_ref, weight_ref, *refs):
    *others, out_ref = refs
    difference = difference_ref[...]
    pairwise = None
    for other_ref in others:
        part = smooth_slope(difference - other_ref[...].astype(f32))
        pairwise = part if pairwise is None else pairwise + part
    out_ref[:, 0, :] = partial_ref[...] - pairwise * weight_ref[...]


def spec():
    return pl.BlockSpec(memory_space=VMEM)


def far():
    return pl.BlockSpec(memory_space=pltpu.HBM)


def scalar():
    return pl.BlockSpec(memory_space=pltpu.SMEM)


def shape(*dims, dtype=bf16):
    return jax.ShapeDtypeStruct(dims, dtype)


def call(kernel, name, scalars, operands, outs, scratch, flops, from_hbm=False):
    moved = sum(o.size * o.dtype.itemsize for o in (*operands, *outs))
    return pl.pallas_call(
        kernel,
        name=name,
        out_shape=outs,
        in_specs=[scalar()] * len(scalars) + [far() if from_hbm else spec()] * len(operands),
        out_specs=tuple(spec() for _ in outs),
        scratch_shapes=scratch,
        compiler_params=pltpu.CompilerParams(vmem_limit_bytes=24 * 2**20),
        cost_estimate=pl.CostEstimate(flops=flops, bytes_accessed=moved, transcendentals=0),
    )(*scalars, *operands)


def exchange(pair_rows, cross_rows):
    members, bands = lax.axis_size("mem"), lax.axis_size("patch")
    pair = [(i, i ^ 1) for i in range(bands)]
    cross = []
    for m in range(members):
        for i in range(bands):
            j = ((i + 1) ^ 1) - 1
            other = (m, j) if 0 <= j < bands else (m ^ 1, i)
            cross.append((m * bands + i, other[0] * bands + other[1]))
    crossed = lax.ppermute(cross_rows, ("mem", "patch"), cross)
    return lax.ppermute(pair_rows, "patch", pair), crossed


def mate(rows):
    members = lax.axis_size("mem")
    return lax.ppermute(rows, "mem", [(m, m ^ 1) for m in range(members)])


def chip_mates(rows):
    members = lax.axis_size("mem")
    far_own = [
        lax.ppermute(rows, "mem", [(m, (m + shift) % members) for m in range(members)])
        for shift in range(2, members, 2)
    ]
    return mate(rows), far_own


def per_device(
    mesh_latent,
    edge_latent,
    grid_edge_latent,
    edge_inner,
    edge_outer,
    node_inner,
    node_outer,
    grid_inner,
    grid_outer,
    out_weight,
    prior_state,
    target,
    channel_weight,
    area_weight,
    send_rows,
    edge_senders,
    edge_receivers,
    edge_count,
    grid_senders,
):
    latent = mesh_latent[0]
    sends = send_rows[0]
    halo = sends.shape[1]
    nodes, width = latent.shape
    edges = edge_senders.shape[0]
    grid_edges = grid_senders.shape[0]
    channels, points = prior_state.shape
    senders = edge_senders
    receivers = edge_receivers
    grid_rows = grid_senders

    pair, cross = call(
        select_kernel,
        "select",
        (),
        tuple(pltpu.with_memory_space_constraint(x, pltpu.HBM) for x in (sends, latent)),
        (shape(halo, width), shape(halo, width)),
        (VMEM((2, halo), jnp.int32), VMEM((nodes, width), bf16), pltpu.SemaphoreType.DMA((3,))),
        10**10,
        from_hbm=True,
    )
    pair_in, cross_in = exchange(pair, cross)
    pre, sent_pre, outer, second, choice, live, sent_placing = call(
        lambda *refs: edge_own_kernel(edges, *refs),
        "edge_own",
        (),
        (
            edge_count,
            sends,
            senders,
            receivers,
            pair,
            cross,
            latent,
            edge_latent,
            edge_inner,
            edge_outer,
            node_inner,
            node_outer,
        ),
        (
            shape(edges, width, dtype=f32),
            shape(2 * halo, width, dtype=f32),
            shape(width, width),
            shape(width, width),
            shape(edges, 2 * halo),
            shape(1, edges, dtype=jnp.int32),
            shape(2 * halo, edges),
        ),
        (VMEM((nodes, width), bf16), VMEM((nodes, width), bf16)),
        10**10,
    )
    message, pair, cross, node_pre = call(
        lambda *refs: message_kernel(edges, *refs),
        "message",
        (),
        (
            choice,
            sent_placing,
            pre,
            pair_in,
            cross_in,
            pair,
            cross,
            edge_inner,
            outer,
            sent_pre,
            node_inner,
            second,
            latent,
        ),
        (
            shape(edges, width),
            shape(halo, width),
            shape(halo, width),
            shape(nodes, width, dtype=f32),
        ),
        (VMEM((2 * halo, width), bf16),),
        10**10,
    )
    pair_in, cross_in = exchange(pair, cross)
    pre, outer, choice = call(
        lambda *refs: grid_own_kernel(grid_edges // 2, halo, *refs),
        "grid_own",
        (),
        (
            grid_rows,
            live,
            message,
            latent,
            node_pre,
            node_inner,
            second,
            grid_edge_latent,
            grid_inner,
            grid_outer,
        ),
        (shape(grid_edges, width, dtype=f32), shape(width, width), shape(grid_edges, 2 * halo)),
        (VMEM((nodes, width), bf16),),
        10**10,
    )
    difference, rounded = call(
        lambda *refs: grid_kernel(grid_edges, *refs),
        "grid",
        (),
        (choice, pre, pair_in, cross_in, grid_inner, outer, out_weight, prior_state, target),
        (shape(channels, points, dtype=f32), shape(channels, points)),
        (VMEM((2 * halo, width), bf16), VMEM((width // LANES, grid_edges, LANES), f32)),
        10**10,
    )
    near, far_own = chip_mates(rounded)
    partial, weight = call(
        score_kernel,
        "score",
        (),
        (channel_weight[None], area_weight[None], difference, near, *far_own),
        (shape(channels, points, dtype=f32), shape(channels, points, dtype=f32)),
        (),
        10**8,
    )
    (gradient,) = call(
        finish_kernel,
        "finish",
        (),
        (difference, partial, weight, *(mate(rows) for rows in far_own)),
        (shape(channels, 1, points, dtype=f32),),
        (),
        10**7,
    )
    return jnp.transpose(gradient, (1, 0, 2))


def solution(mesh):
    in_specs = (
        P("mem", "patch", None),
        P("patch", None),
        P("patch", None),
        P(),
        P(),
        P(),
        P(),
        P(),
        P(),
        P(),
        P(None, "patch"),
        P(None, "patch"),
        P(),
        P("patch"),
        P("patch", None, None),
        P("patch"),
        P("patch"),
        P("patch"),
        P("patch"),
    )
    out_specs = P("mem", None, "patch")
    return jax.shard_map(
        per_device, mesh=mesh, in_specs=in_specs, out_specs=out_specs, check_vma=False
    )
```
